512 devices in a mesh: tile: 128 (over z, y_hi, x), trc: 4 (over y_lo, core).
Axes of the slice: x: 4, y: 4 (y_hi: 2, y_lo: 2; y = y_hi * 2 + y_lo), z: 16, core: 2. Of those that a mesh axis runs over, the one named last changes fastest.
Arguments:
- tracers: float32 [256, 4, 512, 128], P('trc', None, 'tile'), may hold values from 0.1 to 4
- courant_cycle: float32 [4, 512, 128], P(None, 'tile'), may hold values from -0.45 to 0.45
- courant_edge: float32 [4, 512, 128], P(None, 'tile'), may hold values from -0.45 to 0.45
- seam_flags: int32 [128, 2], P('tile'), may hold values from 0 to 1, as said below
- sunlit: int32 [512, 128], P('tile', 'trc'), may hold values from 0 to 1, as said below
- table_entry: int32 [4, 4, 512, 128], P(None, None, 'tile', 'trc'), may hold values from 0 to 3
- linear_maps: bfloat16 [4, 256, 256], replicated, may hold values from -0.375 to 0.375
- offsets: float32 [4, 256], replicated, may hold values from -4 to 4
- mixing: float32 [3, 512, 128], P(None, 'tile', 'trc'), may hold values from 0.05 to 5
Outputs:
- tracers_out: float32 [256, 4, 512, 128], P('trc', None, 'tile')
The draws below stay inside these ranges and needn't reach their ends.
Inputs may be any that keep to these rules, and one draw needn't show every extreme that they name: seam_flags[t, 1] equals seam_flags[t + 1, 0] (tile numbers mod 128); a flag is 1 only on the edge before a tile whose number is a multiple of 32, and at least one flag is 1. In every row of the edge-cell dimension, cycle column x is sunlit exactly when cycle column x + 512 / 2 (mod 512) is not; some tile is sunlit in all of its columns.
All inputs are finite; a program needn't handle non-finite values.
Results may differ from the reference program's by a relative error of at most 0.0025.
Values may be sent and summed in bfloat16 or wider, within the bound.
No kernel may reach another device: no remote copies, remote signals or barrier semaphores. Data moves between devices by JAX's collectives and lax.ppermute only.
A program may use at most 64 MiB of HBM per device.

```python
import math
import jax
import jax.numpy as jnp
from jax import lax

SPECIES = 256
LEVELS = 4
EDGE_CELLS = 128
TILE_COLS = 4
SUBSTEPS = 4
ENTRIES = 4
TILES = 128
CYCLE_COLS = 512


def draw_seam_flags(key, part):
    tile_index = jnp.arange(TILES, dtype=jnp.int32)
    face_start = tile_index % (TILES // 4) == 0
    edge_flags = jax.random.randint(jax.random.fold_in(key, 11), (TILES,), 0, 2)
    forced = jax.random.randint(jax.random.fold_in(key, 12), (), 0, 4) * (TILES // 4)
    edge_flags = jnp.where(tile_index == forced, 1, edge_flags)
    edge_flags = jnp.where(face_start, edge_flags, 0).astype(jnp.int32)
    return jnp.stack([edge_flags, jnp.roll(edge_flags, -1)], axis=1)


def draw_sunlit(key, part):
    sun_column = jax.random.randint(jax.random.fold_in(key, 21), (), 0, CYCLE_COLS)
    row_offset = jax.random.randint(jax.random.fold_in(key, 22), (EDGE_CELLS,), 0, TILE_COLS)
    cycle_index = jnp.arange(CYCLE_COLS, dtype=jnp.int32)
    phase = (cycle_index[:, None] - sun_column + row_offset[None, :]) % CYCLE_COLS
    return (phase < CYCLE_COLS // 2).astype(jnp.int32)


def touch_ends(values, own_key, least, high):
    longest = values.shape.index(max(values.shape))
    spots = []
    for shift in (0, 1):
        where = [jax.random.randint(jax.random.fold_in(own_key, axis), (), 0, length) for axis, length in enumerate(values.shape)]
        where[longest] = (where[longest] + shift) % values.shape[longest]
        spots.append(tuple(where))
    return values.at[spots[0]].set(least).at[spots[1]].set(high)


def steps_of(stream_key, dims, shards, smallest, largest):
    def one(dim, blocks):
        heights = jax.random.uniform(jax.random.fold_in(jax.random.fold_in(stream_key, 6), dim), (blocks,), jnp.float32, smallest / len(shards), largest / len(shards))
        return jnp.repeat(jnp.exp(heights), dims[dim] // blocks).reshape((-1,) + (1,) * (len(dims) - dim - 1))

    gain = one(*shards[0])
    for cut in shards[1:]:
        gain = gain * one(*cut)
    return gain


def bell_draw(key, shape, width, limit, kind=jnp.bfloat16):
    array = width * jax.random.normal(key, shape, jnp.float32)
    return jnp.clip(array, min=-limit, max=limit).astype(kind)


def setup_inputs(seed: int = 0) -> dict:
    arg_keys = jax.random.split(jax.random.key(seed), 10)
    return {
        "tracers": jnp.clip(jnp.exp(math.log(4.0) - 3.6888794 * jax.random.uniform(arg_keys[0], (SPECIES, LEVELS, CYCLE_COLS, EDGE_CELLS), jnp.float32) ** steps_of(arg_keys[0], (SPECIES, LEVELS, CYCLE_COLS, EDGE_CELLS), ((0, 4), (2, 128)), -0.2, 0.2)), 0.1, 4.0),
        "courant_cycle": jnp.clip(jax.random.uniform(arg_keys[1], (LEVELS, CYCLE_COLS, EDGE_CELLS), jnp.float32, -0.45, 0.45) * steps_of(arg_keys[1], (LEVELS, CYCLE_COLS, EDGE_CELLS), ((1, 128),), -0.4, 0.0), -0.45, 0.45),
        "courant_edge": jnp.clip(jax.random.uniform(arg_keys[2], (LEVELS, CYCLE_COLS, EDGE_CELLS), jnp.float32, -0.45, 0.45) * steps_of(arg_keys[2], (LEVELS, CYCLE_COLS, EDGE_CELLS), ((1, 128),), -0.4, 0.0), -0.45, 0.45),
        "seam_flags": draw_seam_flags(jax.random.fold_in(arg_keys[9], 71), 0),
        "sunlit": draw_sunlit(jax.random.fold_in(arg_keys[9], 71), 0),
        "table_entry": touch_ends(jax.random.randint(arg_keys[5], (SUBSTEPS, LEVELS, CYCLE_COLS, EDGE_CELLS), 0, ENTRIES), jax.random.fold_in(arg_keys[5], 1), 0, ENTRIES - 1).astype(jnp.int32),
        "linear_maps": bell_draw(arg_keys[6], (ENTRIES, SPECIES, SPECIES), SPECIES ** -0.5, 0.375),
        "offsets": bell_draw(arg_keys[7], (ENTRIES, SPECIES), 0.7, 4.0, jnp.float32),
        "mixing": jnp.clip(jnp.exp(math.log(5.0) - 4.6051702 * jax.random.uniform(arg_keys[8], (LEVELS - 1, CYCLE_COLS, EDGE_CELLS), jnp.float32) ** steps_of(arg_keys[8], (LEVELS - 1, CYCLE_COLS, EDGE_CELLS), ((1, 128), (2, 4)), -0.2, 0.2)), 0.05, 5.0),
    }


def cut_range(values, start, stop, direction):
    return lax.slice_in_dim(values, start, stop, axis=direction)


def edge_values(stencil, direction):
    length = stencil.shape[direction]
    inner_sum = cut_range(stencil, 1, length - 2, direction) + cut_range(stencil, 2, length - 1, direction)
    outer_sum = cut_range(stencil, 0, length - 3, direction) + cut_range(stencil, 3, length, direction)
    return (7.0 / 12.0) * inner_sum - (1.0 / 12.0) * outer_sum


def sweep_flux(stencil, courant, direction):
    inside = stencil.shape[direction] - 6
    edge_vals = edge_values(stencil, direction)
    left_pos = cut_range(edge_vals, 0, inside + 1, direction)
    middle = cut_range(edge_vals, 1, inside + 2, direction)
    right_neg = cut_range(edge_vals, 2, inside + 3, direction)
    center_pos = cut_range(stencil, 2, inside + 3, direction)
    center_neg = cut_range(stencil, 3, inside + 4, direction)
    curve_pos = 6.0 * center_pos - 3.0 * (left_pos + middle)
    flux_pos = courant * (middle - 0.5 * courant * ((middle - left_pos) - (1.0 - 2.0 * courant / 3.0) * curve_pos))
    reverse_speed = -courant
    curve_neg = 6.0 * center_neg - 3.0 * (middle + right_neg)
    flux_neg = courant * (middle + 0.5 * reverse_speed * ((right_neg - middle) + (1.0 - 2.0 * reverse_speed / 3.0) * curve_neg))
    return jnp.where(courant > 0.0, flux_pos, flux_neg)


def tendency(flux, direction):
    length = flux.shape[direction]
    return cut_range(flux, 0, length - 1, direction) - cut_range(flux, 1, length, direction)


def wall_faces(courant_edge):
    closed = jnp.zeros(courant_edge.shape[:-1] + (1,), jnp.float32)
    return jnp.concatenate([closed, courant_edge[..., 1:], closed], axis=-1)


def edge_sweep(tracers, courant_edge):
    stencil = jnp.pad(tracers, ((0, 0), (0, 0), (0, 0), (3, 3)), mode="edge")
    return tendency(sweep_flux(stencil, wall_faces(courant_edge)[None], 3), 3)


def solve_columns(values, coupling):
    levels = values.shape[1]
    zero_row = jnp.zeros(values.shape[2:], jnp.float32)
    ratio_list = []
    solved_list = []
    for level_index in range(levels):
        coupling_below = coupling[level_index - 1] if level_index > 0 else zero_row
        coupling_above = coupling[level_index] if level_index < levels - 1 else zero_row
        diagonal = 1.0 + coupling_below + coupling_above
        if level_index == 0:
            pivot_value = diagonal
            current = values[:, 0] / pivot_value
        else:
            pivot_value = diagonal - coupling_below * ratio_list[-1]
            current = (values[:, level_index] + coupling_below * solved_list[-1]) / pivot_value
        ratio_list.append(coupling_above / pivot_value)
        solved_list.append(current)
    result_list = [solved_list[-1]]
    for level_index in range(levels - 2, -1, -1):
        result_list.append(solved_list[level_index] + ratio_list[level_index] * result_list[-1])
    return jnp.stack(result_list[::-1], axis=1)


def chemistry_steps(rounded, entry_ids, linear_maps, offsets):
    chem_input = rounded
    result = rounded.astype(jnp.float32)
    for substep in range(entry_ids.shape[0]):
        summed = jnp.zeros(rounded.shape, jnp.float32)
        for entry_id in range(linear_maps.shape[0]):
            product = jnp.dot(linear_maps[entry_id].astype(jnp.float32), chem_input.astype(jnp.float32), precision=lax.Precision.HIGHEST)
            summed = jnp.where(entry_ids[substep][None, :] == entry_id, product + offsets[entry_id][:, None], summed)
        result = jnp.maximum(summed, 0.0)
        chem_input = result.astype(jnp.bfloat16)
    return result


def reference(tracers, courant_cycle, courant_edge, seam_flags, sunlit, table_entry, linear_maps, offsets, mixing):
    species, levels, cycle_length, edge_length = tracers.shape
    courant_tiles = courant_cycle.reshape(levels, TILES, TILE_COLS, edge_length)
    next_face = jnp.roll(courant_tiles, -1, axis=1)[:, :, :1, :]
    flip_next = (seam_flags[:, 1] > 0).reshape(1, TILES, 1, 1)
    next_face = jnp.where(flip_next, next_face[..., ::-1], next_face)
    cycle_faces = jnp.concatenate([courant_tiles, next_face], axis=2)
    flip_before = (seam_flags[:, 0] > 0).reshape(1, 1, TILES, 1, 1)
    flip_after = (seam_flags[:, 1] > 0).reshape(1, 1, TILES, 1, 1)

    def advect(group):
        tiled = group.reshape(group.shape[0], levels, TILES, TILE_COLS, edge_length)
        before = jnp.roll(tiled, 1, axis=2)[:, :, :, -3:, :]
        after_cols = jnp.roll(tiled, -1, axis=2)[:, :, :, :3, :]
        before = jnp.where(flip_before, before[..., ::-1], before)
        after_cols = jnp.where(flip_after, after_cols[..., ::-1], after_cols)
        stencil = jnp.concatenate([before, tiled, after_cols], axis=3)
        cycle_part = tendency(sweep_flux(stencil, cycle_faces[None], 3), 3).reshape(group.shape)
        return group + cycle_part + edge_sweep(group, courant_edge)

    group_size = 8
    grouped = tracers.reshape(species // group_size, group_size, levels, cycle_length, edge_length)
    advected = lax.map(advect, grouped).reshape(tracers.shape)
    rounded = advected.astype(jnp.bfloat16)

    conc_tiles = jnp.moveaxis(rounded.reshape(species, levels, TILES, TILE_COLS, edge_length), 2, 0)
    entry_tiles = jnp.moveaxis(table_entry.reshape(table_entry.shape[0], levels, TILES, TILE_COLS, edge_length), 2, 0)
    sun_tiles = sunlit.reshape(TILES, TILE_COLS * edge_length)
    mixing_tiles = jnp.moveaxis(mixing.reshape(levels - 1, TILES, TILE_COLS, edge_length), 1, 0)

    def column_work(pieces):
        conc_tile, entry_tile, sun_tile, mixing_tile = pieces
        columns = TILE_COLS * edge_length
        flat = conc_tile.reshape(species, levels * columns)
        changed = chemistry_steps(flat, entry_tile.reshape(entry_tile.shape[0], levels * columns), linear_maps, offsets)
        daylight = jnp.broadcast_to(sun_tile[None, :] > 0, (levels, columns)).reshape(levels * columns)
        chem_out = jnp.where(daylight[None, :], changed, flat.astype(jnp.float32)).reshape(species, levels, columns)
        return solve_columns(chem_out, mixing_tile.reshape(levels - 1, columns))

    mixed_out = lax.map(column_work, (conc_tiles, entry_tiles, sun_tiles, mixing_tiles))
    mixed_out = mixed_out.reshape(TILES, species, levels, TILE_COLS, edge_length)
    return jnp.moveaxis(mixed_out, 0, 2).reshape(tracers.shape)
```

```python
import functools

import jax
import jax.numpy as jnp
from jax import lax
from jax.experimental import pallas as pl
from jax.experimental.pallas import tpu as pltpu
from jax.sharding import PartitionSpec as P

F32 = jnp.float32
BF16 = jnp.bfloat16
LANES = 128
CHUNK = 16


def vmem():
    return pl.BlockSpec(memory_space=pltpu.VMEM)


def smem():
    return pl.BlockSpec(memory_space=pltpu.SMEM)


def params(mib):
    return pltpu.CompilerParams(vmem_limit_bytes=mib << 20)


def flux_weights(courant):
    speed = jnp.abs(courant)
    rest = 1.0 - speed
    return (
        courant * rest * rest,
        -courant * speed * rest,
        courant * speed * (3.0 - 2.0 * speed),
        courant > 0.0,
    )


def edge_value(outer_low, inner_low, inner_high, outer_high):
    return (7.0 / 12.0) * (inner_low + inner_high) - (1.0 / 12.0) * (outer_low + outer_high)


def face_flux(weights, values_low, values_mid, values_high, cell_low, cell_high):
    w_mid, w_far, w_centre, positive = weights
    far = jnp.where(positive, values_low, values_high)
    centre = jnp.where(positive, cell_low, cell_high)
    return w_mid * values_mid + w_far * far + w_centre * centre


def block_transpose(rows, lane):
    low = lane < 64
    even = (lane & 32) == 0
    r0, r1, r2, r3 = rows
    b0 = jnp.where(low, r0, pltpu.roll(r2, 64, 1))
    b2 = jnp.where(low, pltpu.roll(r0, 64, 1), r2)
    b1 = jnp.where(low, r1, pltpu.roll(r3, 64, 1))
    b3 = jnp.where(low, pltpu.roll(r1, 64, 1), r3)
    return (
        jnp.where(even, b0, pltpu.roll(b1, 32, 1)),
        jnp.where(even, pltpu.roll(b0, 96, 1), b1),
        jnp.where(even, b2, pltpu.roll(b3, 32, 1)),
        jnp.where(even, pltpu.roll(b2, 96, 1), b3),
    )


def pack_kernel(levels, width, quarter, x_ref, u_ref, next_ref, prev_ref):
    grid = levels * width
    for level in range(levels):
        for col in range(width):
            values = x_ref[pl.ds(level * width + col, quarter, stride=grid), :].astype(BF16)
            if col >= width - 3:
                row = (level * 3 + col - (width - 3)) * quarter
                next_ref[row : row + quarter, :] = values
            if col < 3:
                row = (level * 3 + col) * quarter
                prev_ref[row : row + quarter, :] = values
    first = u_ref[pl.ds(0, levels, stride=width), :]
    high = first.astype(BF16).astype(F32)
    rest = first - high
    mid = rest.astype(BF16).astype(F32)
    low = rest - mid
    row = levels * 3 * quarter
    parts = jnp.concatenate([high, mid, low, jnp.zeros_like(low)], axis=0)
    prev_ref[row : row + 4 * levels, :] = parts.astype(BF16)


def edge_kernel(levels, width, quarter, x_ref, u_ref, base_ref):
    grid = levels * width
    lane = lax.broadcasted_iota(jnp.int32, (CHUNK, LANES), 1)
    first = lane == 0
    last = lane == LANES - 1
    for cell in range(grid):
        courant = jnp.where(first, 0.0, jnp.broadcast_to(u_ref[cell : cell + 1, :], lane.shape))
        weights = flux_weights(courant)
        for start in range(0, quarter, CHUNK):
            x = x_ref[pl.ds(start * grid + cell, CHUNK, stride=grid), :]
            below = jnp.where(first, x, pltpu.roll(x, 1, 1))
            below2 = jnp.where(first, below, pltpu.roll(below, 1, 1))
            above = jnp.where(last, x, pltpu.roll(x, LANES - 1, 1))
            mid = edge_value(below2, below, x, above)
            end = (13.0 / 12.0) * x - (1.0 / 12.0) * below
            after = jnp.where(last, end, pltpu.roll(mid, LANES - 1, 1))
            flux = face_flux(weights, pltpu.roll(mid, 1, 1), mid, after, below, x)
            base_ref[cell, start : start + CHUNK, :] = x + (flux - pltpu.roll(flux, LANES - 1, 1))


def flow_kernel(
    levels, width, quarter, flag_ref, x_ref, base_ref, u_ref, before_ref, after_ref, out_ref
):
    grid = levels * width
    lane = lax.broadcasted_iota(jnp.int32, (CHUNK, LANES), 1)
    turn_before = jnp.where(flag_ref[0, 0] > 0, LANES - 1 - lane, lane)
    turn_after = jnp.where(flag_ref[0, 1] > 0, LANES - 1 - lane, lane)
    tail = levels * 3 * quarter
    split = after_ref[tail : tail + 4 * levels, :].astype(F32)
    split = jnp.take_along_axis(split, turn_after, axis=1)
    closing = split[0:levels] + split[levels : 2 * levels] + split[2 * levels : 3 * levels]
    for level in range(levels):
        faces = [u_ref[level * width + f : level * width + f + 1, :] for f in range(width)]
        faces.append(closing[level : level + 1, :])
        weights = [flux_weights(jnp.broadcast_to(f, lane.shape)) for f in faces]
        for start in range(0, quarter, CHUNK):
            cells = []
            for col in range(3):
                row = (level * 3 + col) * quarter + start
                halo = before_ref[row : row + CHUNK, :].astype(F32)
                cells.append(jnp.take_along_axis(halo, turn_before, axis=1))
            for col in range(width):
                cells.append(
                    x_ref[pl.ds(start * grid + level * width + col, CHUNK, stride=grid), :]
                )
            for col in range(3):
                row = (level * 3 + col) * quarter + start
                halo = after_ref[row : row + CHUNK, :].astype(F32)
                cells.append(jnp.take_along_axis(halo, turn_after, axis=1))
            values = [edge_value(*cells[i : i + 4]) for i in range(width + 3)]
            fluxes = [
                face_flux(weights[f], *values[f : f + 3], cells[f + 2], cells[f + 3])
                for f in range(width + 1)
            ]
            moved = [
                base_ref[level * width + col, start : start + CHUNK, :]
                + (fluxes[col] - fluxes[col + 1])
                for col in range(width)
            ]
            for part, rows in enumerate(block_transpose(moved, lane)):
                out_ref[part, level, start : start + CHUNK, :] = rows.astype(BF16)


def chem_kernel(
    levels, quarter, x_ref, entry_ref, sun_ref, mix_ref, map_ref, off_ref, out_ref, chem_ref
):
    parts = x_ref.shape[0]
    species = parts * quarter
    entries = map_ref.shape[0] // species
    substeps = entry_ref.shape[0] // levels
    halves = levels // 2
    start = []
    for half in range(halves):
        pair = [
            jnp.concatenate([x_ref[p, 2 * half + k] for p in range(parts)], axis=0)
            for k in range(2)
        ]
        start.append(jnp.concatenate(pair, axis=1))
    state = list(start)
    result = [None] * halves
    for step in range(substeps):
        for half in range(halves):
            product = jnp.dot(map_ref[...], state[half], preferred_element_type=F32)
            row = step * levels + 2 * half
            entry = jnp.concatenate(
                [entry_ref[row : row + 1, :], entry_ref[row + 1 : row + 2, :]], axis=1
            )
            chosen = product[0:species] + off_ref[:, 0:1]
            for e in range(1, entries):
                chosen = jnp.where(
                    entry == e,
                    product[e * species : (e + 1) * species] + off_ref[:, e : e + 1],
                    chosen,
                )
            result[half] = jnp.maximum(chosen, 0.0)
            state[half] = result[half].astype(BF16)
    lit = jnp.concatenate([sun_ref[...], sun_ref[...]], axis=1) > 0
    for half in range(halves):
        chem = jnp.where(lit, result[half], start[half].astype(F32))
        chem_ref[2 * half] = chem[:, 0:LANES]
        chem_ref[2 * half + 1] = chem[:, LANES : 2 * LANES]
    mixing = [mix_ref[k : k + 1, :] for k in range(levels - 1)]
    inverse, ratio = [], []
    for level in range(levels):
        diagonal = 1.0
        if level > 0:
            diagonal = diagonal + mixing[level - 1]
        if level < levels - 1:
            diagonal = diagonal + mixing[level]
        if level > 0:
            diagonal = diagonal - mixing[level - 1] * ratio[level - 1]
        inverse.append(1.0 / diagonal)
        if level < levels - 1:
            ratio.append(mixing[level] * inverse[level])
    for p in range(parts):
        for begin in range(0, quarter, CHUNK):
            rows = slice(p * quarter + begin, p * quarter + begin + CHUNK)
            solved = []
            for level in range(levels):
                value = chem_ref[level, rows, :]
                if level > 0:
                    value = value + mixing[level - 1] * solved[-1]
                solved.append(value * inverse[level])
            for level in range(levels - 2, -1, -1):
                solved[level] = solved[level] + ratio[level] * solved[level + 1]
            for level in range(levels):
                out_ref[p, level, begin : begin + CHUNK, :] = solved[level].astype(BF16)


def unpack_kernel(levels, width, quarter, y_ref, out_ref):
    grid = levels * width
    lane = lax.broadcasted_iota(jnp.int32, (CHUNK, LANES), 1)
    for level in range(levels):
        for start in range(0, quarter, CHUNK):
            rows = [y_ref[q, level, start : start + CHUNK, :].astype(F32) for q in range(4)]
            for col, values in enumerate(block_transpose(rows, lane)):
                out_ref[pl.ds(start * grid + level * width + col, CHUNK, stride=grid), :] = values


def shards(
    tracers,
    courant_cycle,
    courant_edge,
    seam_flags,
    sunlit,
    table_entry,
    linear_maps,
    offsets,
    mixing,
):
    quarter, levels, width, length = tracers.shape
    grid = levels * width
    substeps = table_entry.shape[0]
    entries, species, _ = linear_maps.shape
    count = lax.axis_size("tile")
    parts = lax.axis_size("trc")
    forward = [(i, (i + 1) % count) for i in range(count)]
    backward = [(target, source) for source, target in forward]
    x = tracers.reshape(quarter * grid, length)
    cycle = courant_cycle.reshape(grid, length)
    halo = levels * 3 * quarter
    to_next, to_prev = pl.pallas_call(
        functools.partial(pack_kernel, levels, width, quarter),
        out_shape=(
            jax.ShapeDtypeStruct((halo, length), BF16),
            jax.ShapeDtypeStruct((halo + 4 * levels, length), BF16),
        ),
        in_specs=[vmem()] * 2,
        out_specs=(vmem(), vmem()),
        compiler_params=params(8),
        name="pack",
    )(x, cycle)
    before = lax.ppermute(to_next, "tile", forward)
    after = lax.ppermute(to_prev, "tile", backward)
    base = pl.pallas_call(
        functools.partial(edge_kernel, levels, width, quarter),
        out_shape=jax.ShapeDtypeStruct((grid, quarter, length), F32),
        in_specs=[vmem()] * 2,
        out_specs=vmem(),
        compiler_params=params(8),
        cost_estimate=pl.CostEstimate(flops=4000000, bytes_accessed=1 << 20, transcendentals=0),
        name="edge",
    )(x, courant_edge.reshape(grid, length))
    moved = pl.pallas_call(
        functools.partial(flow_kernel, levels, width, quarter),
        out_shape=jax.ShapeDtypeStruct((parts, levels, quarter, length), BF16),
        in_specs=[smem()] + [vmem()] * 5,
        out_specs=vmem(),
        compiler_params=params(8),
        name="flow",
    )(seam_flags, x, base, cycle, before, after)
    boxes = lax.all_to_all(moved, "trc", split_axis=0, concat_axis=0, tiled=True)
    mixed = pl.pallas_call(
        functools.partial(chem_kernel, levels, quarter),
        out_shape=jax.ShapeDtypeStruct((parts, levels, quarter, length), BF16),
        in_specs=[vmem()] * 6,
        out_specs=vmem(),
        scratch_shapes=[pltpu.VMEM((levels, species, length), F32)],
        compiler_params=params(24),
        name="chem",
    )(
        boxes,
        table_entry.reshape(substeps * levels, length),
        sunlit.reshape(1, length),
        mixing.reshape(levels - 1, length),
        linear_maps.reshape(entries * species, species),
        offsets.T,
    )
    back = lax.all_to_all(mixed, "trc", split_axis=0, concat_axis=0, tiled=True)
    out = pl.pallas_call(
        functools.partial(unpack_kernel, levels, width, quarter),
        out_shape=jax.ShapeDtypeStruct((quarter * grid, length), F32),
        in_specs=[vmem()],
        out_specs=vmem(),
        compiler_params=params(8),
        name="unpack",
    )(back)
    return out.reshape(quarter, levels, width, length)


def solution(mesh):
    placed = (
        P("trc", None, "tile", None),
        P(None, "tile", None),
        P(None, "tile", None),
        P("tile", None),
        P("tile", "trc"),
        P(None, None, "tile", "trc"),
        P(),
        P(),
        P(None, "tile", "trc"),
    )
    return jax.shard_map(
        shards, mesh=mesh, in_specs=placed, out_specs=P("trc", None, "tile", None), check_vma=False
    )
```

```python
import functools

import jax
import jax.numpy as jnp
from jax import lax
from jax.experimental import pallas as pl
from jax.experimental.pallas import tpu as pltpu
from jax.sharding import PartitionSpec as P

F32 = jnp.float32
BF16 = jnp.bfloat16
LANES = 128
TABLE_ROWS = 32


def vmem():
    return pl.BlockSpec(memory_space=pltpu.VMEM)


def smem():
    return pl.BlockSpec(memory_space=pltpu.SMEM)


def hbm():
    return pl.BlockSpec(memory_space=pltpu.HBM)


def in_hbm(array):
    return pltpu.with_memory_space_constraint(array, pltpu.HBM)


def params(mib):
    return pltpu.CompilerParams(vmem_limit_bytes=mib << 20)


def face_weights(courant):
    speed = jnp.abs(courant)
    rest = 1.0 - speed
    mid = courant * rest * rest
    far = -courant * speed * rest
    centre = courant * speed * (3.0 - 2.0 * speed)
    positive = courant > 0.0
    far_low = jnp.where(positive, far, 0.0)
    far_high = far - far_low
    centre_low = jnp.where(positive, centre, 0.0)
    centre_high = centre - centre_low
    small, large = 1.0 / 12.0, 7.0 / 12.0
    return [
        -small * far_low,
        large * far_low - small * mid,
        large * (mid + far_low) - small * far_high + centre_low,
        large * (mid + far_high) - small * far_low + centre_high,
        large * far_high - small * mid,
        -small * far_high,
    ]


def cell_weights(before, after):
    zero = jnp.zeros_like(before[0])
    return [a - b for a, b in zip(before + [zero], [zero] + after)]


def block_transpose(rows, lane):
    low = lane < 64
    even = (lane & 32) == 0
    r0, r1, r2, r3 = rows
    b0 = jnp.where(low, r0, pltpu.roll(r2, 64, 1))
    b2 = jnp.where(low, pltpu.roll(r0, 64, 1), r2)
    b1 = jnp.where(low, r1, pltpu.roll(r3, 64, 1))
    b3 = jnp.where(low, pltpu.roll(r1, 64, 1), r3)
    return (
        jnp.where(even, b0, pltpu.roll(b1, 32, 1)),
        jnp.where(even, pltpu.roll(b0, 96, 1), b1),
        jnp.where(even, b2, pltpu.roll(b3, 32, 1)),
        jnp.where(even, pltpu.roll(b2, 96, 1), b3),
    )


def split3(values):
    high = values.astype(BF16).astype(F32)
    rest = values - high
    mid = rest.astype(BF16).astype(F32)
    return high, mid, rest - mid


def pack_kernel(levels, width, quarter, x_hbm, u_hbm, next_ref, prev_ref, x_ref, u_ref, sems):
    grid = levels * width
    pieces = sems.shape[0] - 1
    part = quarter // pieces
    copies = [pltpu.make_async_copy(u_hbm, u_ref, sems.at[pieces])]
    for i in range(pieces):
        rows = pl.ds(i * part * grid, part * grid)
        copies.append(pltpu.make_async_copy(x_hbm.at[rows], x_ref.at[rows], sems.at[i]))
    for copy in copies:
        copy.start()
    copies[0].wait()
    row = levels * 3 * quarter
    parts = split3(u_ref[pl.ds(0, levels, stride=width), :])
    parts = jnp.concatenate(parts + (jnp.zeros_like(parts[0]),), axis=0)
    prev_ref[row : row + 4 * levels, :] = parts.astype(BF16)
    for i in range(pieces):
        copies[1 + i].wait()
        for level in range(levels):
            for col in range(width):
                start = i * part * grid + level * width + col
                values = x_ref[pl.ds(start, part, stride=grid), :].astype(BF16)
                if col >= width - 3:
                    row = (level * 3 + col - (width - 3)) * quarter + i * part
                    next_ref[row : row + part, :] = values
                if col < 3:
                    row = (level * 3 + col) * quarter + i * part
                    prev_ref[row : row + part, :] = values


def local_kernel(
    levels,
    width,
    quarter,
    flag_ref,
    x_ref,
    cycle_ref,
    edge_ref,
    entry_ref,
    sun_ref,
    mix_ref,
    base_ref,
    weight_ref,
    table_ref,
    turn_ref,
    own_ref,
    tab_ref,
):
    grid = levels * width
    chunk = 32
    row = lax.broadcasted_iota(jnp.int32, (LANES, LANES), 0)
    col = lax.broadcasted_iota(jnp.int32, (LANES, LANES), 1)
    for side in range(2):
        source = jnp.where(flag_ref[0, side] > 0, LANES - 1 - col, col)
        turn_ref[side] = jnp.where(row == source, 1.0, 0.0).astype(BF16)
    entries = entry_ref.shape[0]
    tab_ref[...] = jnp.zeros_like(tab_ref)
    tab_ref[0:entries, :] = entry_ref[...].astype(F32)
    tab_ref[entries : entries + 1, :] = sun_ref[...].astype(F32)
    for i, part in enumerate(split3(mix_ref[...])):
        row = entries + 1 + i * (levels - 1)
        tab_ref[row : row + levels - 1, :] = part
    table_ref[...] = tab_ref[...].astype(BF16)
    shape = (grid, LANES)
    lane = lax.broadcasted_iota(jnp.int32, shape, 1)
    column = lax.broadcasted_iota(jnp.int32, shape, 0) % width
    faces = face_weights(cycle_ref[...])
    after = [jnp.where(column == width - 1, 0.0, pltpu.roll(w, grid - 1, 0)) for w in faces]
    across = cell_weights(faces, after)
    for k in range(7):
        weight_ref[k] = across[k]
    faces = face_weights(jnp.where(lane == 0, 0.0, edge_ref[...]))
    along = cell_weights(faces, [pltpu.roll(w, LANES - 1, 1) for w in faces])
    low3, low2, low1, here, high1, high2, high3 = along
    here = jnp.where(lane == 0, here + low1 + low2 + low3, here)
    low1 = jnp.where(lane == 1, low1 + low2 + low3, low1)
    low2 = jnp.where(lane == 2, low2 + low3, low2)
    here = jnp.where(lane == LANES - 1, here + high1 + high2 + high3, here)
    high1 = jnp.where(lane == LANES - 2, high1 + high2 + high3, high1)
    high2 = jnp.where(lane == LANES - 3, high2 + high3, high2)
    own_ref[0] = jnp.where(lane < 3, 0.0, low3)
    own_ref[1] = jnp.where(lane < 2, 0.0, low2)
    own_ref[2] = jnp.where(lane < 1, 0.0, low1)
    own_ref[3] = 1.0 + here + across[3]
    own_ref[4] = jnp.where(lane > LANES - 2, 0.0, high1)
    own_ref[5] = jnp.where(lane > LANES - 3, 0.0, high2)
    own_ref[6] = jnp.where(lane > LANES - 4, 0.0, high3)
    for level in range(levels):
        for start in range(0, quarter, chunk):
            cells = [
                x_ref[pl.ds(start * grid + level * width + col, chunk, stride=grid), :]
                for col in range(width)
            ]
            for col in range(width):
                cell = level * width + col
                total = cells[col] * own_ref[3, cell : cell + 1, :]
                for k in (-3, -2, -1, 1, 2, 3):
                    moved = pltpu.roll(cells[col], (-k) % LANES, 1)
                    total = total + moved * own_ref[3 + k, cell : cell + 1, :]
                    if 0 <= col + k < width:
                        total = total + cells[col + k] * weight_ref[3 + k, cell : cell + 1, :]
                base_ref[cell, start : start + chunk, :] = total


def maps_kernel(rank_ref, map_ref, off_ref, full_ref, last_ref, shift_ref, scratch_ref):
    rank = rank_ref[0, 0]
    count, quarter, species = full_ref.shape
    parts = species // quarter
    entries = count // parts
    row = lax.broadcasted_iota(jnp.int32, (species, species), 0)
    col = lax.broadcasted_iota(jnp.int32, (species, species), 1)
    shuffle = jnp.where(row == (col ^ (rank * quarter)), 1.0, 0.0).astype(BF16)
    for e in range(entries):
        moved = jnp.dot(map_ref[e], shuffle, preferred_element_type=F32).astype(BF16)
        for k in range(parts):
            scratch_ref[e * parts + k] = moved[k * quarter : (k + 1) * quarter, :]
    for e in range(entries):
        for k in range(parts):
            block = scratch_ref[e * parts + (rank ^ k)]
            full_ref[e * parts + k] = block
            if k == 0:
                last_ref[e] = block
    for k in range(parts):
        shift_ref[k] = off_ref[rank ^ k]


def flow_kernel(
    levels,
    first,
    some,
    width,
    quarter,
    x_ref,
    base_ref,
    weight_ref,
    table_ref,
    turn_ref,
    before_ref,
    after_ref,
    out_ref,
):
    grid = levels * width
    turn_before, turn_after = turn_ref[0], turn_ref[1]
    halo = levels * 3 * quarter
    split = jnp.dot(
        after_ref[halo : halo + 4 * levels, :], turn_after, preferred_element_type=F32
    )
    closing = split[0:levels] + split[levels : 2 * levels] + split[2 * levels : 3 * levels]
    closing = face_weights(closing)
    chunk = 32
    for level in range(first, first + some):
        for start in range(0, quarter, chunk):
            low, high = [], []
            for i in range(3):
                begin = (level * 3 + i) * quarter + start
                low.append(before_ref[begin : begin + chunk, :])
                high.append(after_ref[begin : begin + chunk, :])
            low = jnp.dot(
                jnp.concatenate(low, axis=0), turn_before, preferred_element_type=F32
            )
            high = jnp.dot(
                jnp.concatenate(high, axis=0), turn_after, preferred_element_type=F32
            )
            outer = {i - 3: low[i * chunk : (i + 1) * chunk] for i in range(3)}
            outer.update({width + i: high[i * chunk : (i + 1) * chunk] for i in range(3)})
            for c in range(width):
                cell = level * width + c
                total = base_ref[cell, start : start + chunk, :]
                for k in range(-3, 4):
                    if c + k in outer and not (c == width - 1 and k == 3):
                        total = total + outer[c + k] * weight_ref[3 + k, cell : cell + 1, :]
                if c == width - 1:
                    for k in range(-3, 3):
                        if width + k in outer:
                            value = outer[width + k]
                        else:
                            begin = start * grid + level * width + width + k
                            value = x_ref[pl.ds(begin, chunk, stride=grid), :]
                        total = total - value * closing[3 + k][level : level + 1, :]
                begin = ((level - first) * width + c) * quarter + start
                out_ref[begin : begin + chunk, :] = total.astype(BF16)
    if first == 0:
        begin = some * width * quarter
        out_ref[begin : begin + TABLE_ROWS, :] = table_ref[...]


def tables_of(rank, tails):
    lane = lax.broadcasted_iota(jnp.int32, (TABLE_ROWS, LANES), 1)
    t0, t1, t2, t3 = [t.astype(F32) for t in tails]
    odd = (rank & 1) > 0
    t0, t1 = jnp.where(odd, t1, t0), jnp.where(odd, t0, t1)
    t2, t3 = jnp.where(odd, t3, t2), jnp.where(odd, t2, t3)
    upper = (rank & 2) > 0
    t0, t2 = jnp.where(upper, t2, t0), jnp.where(upper, t0, t2)
    t1, t3 = jnp.where(upper, t3, t1), jnp.where(upper, t1, t3)
    return block_transpose((t0, t1, t2, t3), lane)


def chem_kernel(
    levels, first, some, width, quarter, entries, substeps, last_call, rank_ref, *refs
):
    parts = 4
    species = parts * quarter
    block_refs = refs[0:parts]
    tail_refs = refs[parts : 2 * parts]
    map_ref, last_ref, off_ref = refs[2 * parts : 2 * parts + 3]
    tail = refs[2 * parts + 3 :]
    columns = tables_of(rank_ref[0, 0], [r[...] for r in tail_refs])
    groups = some * width
    tiles = groups // 2

    def row_of(group, index):
        return columns[group % width][index : index + 1, :]

    def pair_of(tile, function):
        return jnp.concatenate([function(2 * tile), function(2 * tile + 1)], axis=1)

    def block(part, group):
        return block_refs[part][group * quarter : (group + 1) * quarter, :]

    start = [
        pair_of(
            tile, lambda g: jnp.concatenate([block(p, g) for p in range(parts)], axis=0)
        )
        for tile in range(tiles)
    ]
    state = list(start)
    result = [None] * tiles
    for step in range(substeps):
        final = step == substeps - 1
        rows = quarter if final else species
        matrix = last_ref[...] if final else map_ref[...]
        for tile in range(tiles):
            product = jnp.dot(matrix, state[tile], preferred_element_type=F32)
            entry = pair_of(
                tile, lambda g: row_of(g, step * levels + first + g // width)
            )
            chosen = product[0:rows] + off_ref[0:rows, 0:1]
            for e in range(1, entries):
                chosen = jnp.where(
                    entry == float(e),
                    product[e * rows : (e + 1) * rows] + off_ref[0:rows, e : e + 1],
                    chosen,
                )
            result[tile] = jnp.maximum(chosen, 0.0)
            if not final:
                state[tile] = result[tile].astype(BF16)
    sun = substeps * levels
    chem_ref = tail[-1]
    for tile in range(tiles):
        lit = pair_of(tile, lambda g: row_of(g, sun)) > 0.0
        chem = jnp.where(lit, result[tile], start[tile][0:quarter].astype(F32))
        chem_ref[2 * tile] = chem[:, 0:LANES]
        chem_ref[2 * tile + 1] = chem[:, LANES : 2 * LANES]
    if not last_call:
        return
    earlier_refs = tail[:-2]
    out_ref = tail[-2]
    grid = levels * width
    chunk = 32
    for col in range(width):
        pieces = [
            columns[col][sun + 1 + i * (levels - 1) : sun + 1 + (i + 1) * (levels - 1), :]
            for i in range(3)
        ]
        mixed = pieces[0] + pieces[1] + pieces[2]
        mixing = [mixed[k : k + 1, :] for k in range(levels - 1)]
        inverse, ratio = [], []
        for level in range(levels):
            diagonal = 1.0
            if level > 0:
                diagonal = diagonal + mixing[level - 1]
            if level < levels - 1:
                diagonal = diagonal + mixing[level]
            if level > 0:
                diagonal = diagonal - mixing[level - 1] * ratio[level - 1]
            inverse.append(1.0 / diagonal)
            if level < levels - 1:
                ratio.append(mixing[level] * inverse[level])
        for begin in range(0, quarter, chunk):
            solved = []
            for level in range(levels):
                source = chem_ref if level >= first else earlier_refs[level // some]
                value = source[(level % some) * width + col, begin : begin + chunk, :]
                if level > 0:
                    value = value + mixing[level - 1] * solved[-1]
                solved.append(value * inverse[level])
            for level in range(levels - 2, -1, -1):
                solved[level] = solved[level] + ratio[level] * solved[level + 1]
            for level in range(levels):
                place = begin * grid + level * width + col
                out_ref[pl.ds(place, chunk, stride=grid), :] = solved[level]


CALLS = 1


def shards(
    tracers,
    courant_cycle,
    courant_edge,
    seam_flags,
    sunlit,
    table_entry,
    linear_maps,
    offsets,
    mixing,
):
    quarter, levels, width, length = tracers.shape
    grid = levels * width
    substeps = table_entry.shape[0]
    entries, species, _ = linear_maps.shape
    count = lax.axis_size("tile")
    parts = lax.axis_size("trc")
    forward = [(i, (i + 1) % count) for i in range(count)]
    backward = [(target, source) for source, target in forward]
    x = tracers.reshape(quarter * grid, length)
    cycle = courant_cycle.reshape(grid, length)
    halo = levels * 3 * quarter
    pieces = 4
    shape = jax.ShapeDtypeStruct
    to_next, to_prev = pl.pallas_call(
        functools.partial(pack_kernel, levels, width, quarter),
        out_shape=(
            shape((halo, length), BF16),
            shape((halo + 4 * levels, length), BF16),
        ),
        in_specs=[hbm()] * 2,
        out_specs=(vmem(), vmem()),
        scratch_shapes=[
            pltpu.VMEM((quarter * grid, length), F32),
            pltpu.VMEM((grid, length), F32),
            pltpu.SemaphoreType.DMA((pieces + 1,)),
        ],
        compiler_params=params(8),
        name="pack",
    )(in_hbm(x), in_hbm(cycle))
    before = lax.ppermute(to_next, "tile", forward)
    after = lax.ppermute(to_prev, "tile", backward)
    rank = lax.axis_index("trc").astype(jnp.int32).reshape(1, 1)
    base, weights, table, turns = pl.pallas_call(
        functools.partial(local_kernel, levels, width, quarter),
        out_shape=(
            shape((grid, quarter, length), F32),
            shape((7, grid, length), F32),
            shape((TABLE_ROWS, length), BF16),
            shape((2, length, length), BF16),
        ),
        in_specs=[smem()] + [vmem()] * 6,
        out_specs=(vmem(),) * 4,
        scratch_shapes=[
            pltpu.VMEM((7, grid, length), F32),
            pltpu.VMEM((TABLE_ROWS, length), F32),
        ],
        compiler_params=params(8),
        cost_estimate=pl.CostEstimate(flops=4000000, bytes_accessed=1 << 20, transcendentals=0),
        name="local",
    )(
        seam_flags,
        x,
        cycle,
        courant_edge.reshape(grid, length),
        table_entry.reshape(substeps * levels, length),
        sunlit.reshape(1, length),
        mixing.reshape(levels - 1, length),
    )
    full, last, shift = pl.pallas_call(
        maps_kernel,
        out_shape=(
            shape((entries * parts, quarter, species), BF16),
            shape((entries, quarter, species), BF16),
            shape((parts, quarter, entries), F32),
        ),
        in_specs=[smem()] + [vmem()] * 2,
        out_specs=(vmem(),) * 3,
        scratch_shapes=[pltpu.VMEM((entries * parts, quarter, species), BF16)],
        compiler_params=params(8),
        cost_estimate=pl.CostEstimate(flops=4000000, bytes_accessed=1 << 20, transcendentals=0),
        name="maps",
    )(rank, linear_maps, offsets.T.reshape(parts, quarter, entries))
    before, after, base, full, last, shift = lax.optimization_barrier(
        (before, after, base, full, last, shift)
    )
    some = levels // CALLS
    chunks = []
    for call in range(CALLS):
        rows = some * width * quarter + (TABLE_ROWS if call == 0 else 0)
        own = pl.pallas_call(
            functools.partial(flow_kernel, levels, call * some, some, width, quarter),
            out_shape=shape((rows, length), BF16),
            in_specs=[vmem()] * 7,
            out_specs=vmem(),
            compiler_params=params(8),
        )(x, base, weights, table, turns, before, after)
        chunks.append([own])
    swap = {k: [(i, i ^ k) for i in range(parts)] for k in (1, 2)}
    for chunk in chunks:
        chunk.append(lax.ppermute(chunk[0], "trc", swap[1]))
        chunk.append(lax.ppermute(chunk[0], "trc", swap[2]))
        chunk.append(lax.ppermute(chunk[2], "trc", swap[1]))
    tails = [c[some * width * quarter :] for c in chunks[0]]
    results = []
    for call, chunk in enumerate(chunks):
        last_call = call == CALLS - 1
        chem_shape = (some * width, quarter, length)
        if last_call:
            out_shape = shape((quarter * grid, length), F32)
            scratch = [pltpu.VMEM(chem_shape, F32)]
        else:
            out_shape = shape(chem_shape, F32)
            scratch = []
        results.append(
            pl.pallas_call(
                functools.partial(
                    chem_kernel,
                    levels,
                    call * some,
                    some,
                    width,
                    quarter,
                    entries,
                    substeps,
                    last_call,
                ),
                out_shape=out_shape,
                in_specs=[smem()] + [vmem()] * (11 + (len(results) if last_call else 0)),
                out_specs=vmem(),
                scratch_shapes=scratch,
                compiler_params=params(24),
            )(
                rank,
                *chunk,
                *tails,
                full.reshape(entries * species, species),
                last.reshape(entries * quarter, species),
                shift.reshape(species, entries),
                *(results if last_call else []),
            )
        )
    return results[-1].reshape(quarter, levels, width, length)


def solution(mesh):
    placed = (
        P("trc", None, "tile", None),
        P(None, "tile", None),
        P(None, "tile", None),
        P("tile", None),
        P("tile", "trc"),
        P(None, None, "tile", "trc"),
        P(),
        P(),
        P(None, "tile", "trc"),
    )
    return jax.shard_map(
        shards, mesh=mesh, in_specs=placed, out_specs=P("trc", None, "tile", None), check_vma=False
    )
```

```python
import functools

import jax
import jax.numpy as jnp
from jax import lax
from jax.experimental import pallas as pl
from jax.experimental.pallas import tpu as pltpu
from jax.sharding import PartitionSpec as P

F32 = jnp.float32
BF16 = jnp.bfloat16
LANES = 128
TABLE_ROWS = 32


def vmem():
    return pl.BlockSpec(memory_space=pltpu.VMEM)


def smem():
    return pl.BlockSpec(memory_space=pltpu.SMEM)


def hbm():
    return pl.BlockSpec(memory_space=pltpu.HBM)


def in_hbm(array):
    return pltpu.with_memory_space_constraint(array, pltpu.HBM)


def params(mib):
    return pltpu.CompilerParams(vmem_limit_bytes=mib << 20)


def face_weights(courant):
    speed = jnp.abs(courant)
    rest = 1.0 - speed
    mid = courant * rest * rest
    far = -courant * speed * rest
    centre = courant * speed * (3.0 - 2.0 * speed)
    positive = courant > 0.0
    far_low = jnp.where(positive, far, 0.0)
    far_high = far - far_low
    centre_low = jnp.where(positive, centre, 0.0)
    centre_high = centre - centre_low
    small, large = 1.0 / 12.0, 7.0 / 12.0
    return [
        -small * far_low,
        large * far_low - small * mid,
        large * (mid + far_low) - small * far_high + centre_low,
        large * (mid + far_high) - small * far_low + centre_high,
        large * far_high - small * mid,
        -small * far_high,
    ]


def cell_weights(before, after):
    zero = jnp.zeros_like(before[0])
    return [a - b for a, b in zip(before + [zero], [zero] + after)]


def block_transpose(rows, lane):
    low = lane < 64
    even = (lane & 32) == 0
    r0, r1, r2, r3 = rows
    b0 = jnp.where(low, r0, pltpu.roll(r2, 64, 1))
    b2 = jnp.where(low, pltpu.roll(r0, 64, 1), r2)
    b1 = jnp.where(low, r1, pltpu.roll(r3, 64, 1))
    b3 = jnp.where(low, pltpu.roll(r1, 64, 1), r3)
    return (
        jnp.where(even, b0, pltpu.roll(b1, 32, 1)),
        jnp.where(even, pltpu.roll(b0, 96, 1), b1),
        jnp.where(even, b2, pltpu.roll(b3, 32, 1)),
        jnp.where(even, pltpu.roll(b2, 96, 1), b3),
    )


def split3(values):
    high = values.astype(BF16).astype(F32)
    rest = values - high
    mid = rest.astype(BF16).astype(F32)
    return high, mid, rest - mid


def pack_kernel(levels, width, quarter, pieces, *refs):
    even = (refs[0][0, 0] & 1) == 0
    refs = refs[1:]
    count = (len(refs) - 3) // 2
    sources, (a_ref, b_ref), targets = refs[:count], refs[count : count + 2], refs[count + 2 : -1]
    sems = refs[-1]
    x_ref, u_ref = targets[0], targets[1]
    grid = levels * width
    part = quarter // pieces
    small, large = [], []
    for i in range(1, count):
        small.append(pltpu.make_async_copy(sources[i], targets[i], sems.at[pieces + i - 1]))
    for i in range(pieces):
        rows = pl.ds(i * part * grid, part * grid)
        large.append(pltpu.make_async_copy(sources[0].at[rows], x_ref.at[rows], sems.at[i]))
    small[0].start()
    for copy in large + small[1:]:
        copy.start()
    small[0].wait()
    row = levels * 3 * quarter
    parts = split3(u_ref[pl.ds(0, levels, stride=width), :])
    parts = jnp.concatenate(parts + (jnp.zeros_like(parts[0]),), axis=0)
    a_ref[row : row + 4 * levels, :] = parts.astype(BF16)
    b_ref[row : row + 4 * levels, :] = parts.astype(BF16)
    for i in range(pieces):
        large[i].wait()
        for level in range(levels):
            start = i * part * grid + level * width
            cells = [x_ref[pl.ds(start + c, part, stride=grid), :] for c in range(width)]
            for c in range(3):
                row = (level * 3 + c) * quarter + i * part
                low, high = cells[c], cells[width - 3 + c]
                a_ref[row : row + part, :] = jnp.where(even, high, low).astype(BF16)
                b_ref[row : row + part, :] = jnp.where(even, low, high).astype(BF16)
    for copy in small[1:]:
        copy.wait()


def local_kernel(
    levels,
    width,
    quarter,
    tile_ref,
    flag_ref,
    x_ref,
    cycle_ref,
    edge_ref,
    entry_ref,
    sun_ref,
    mix_ref,
    base_ref,
    weight_ref,
    table_ref,
    turn_ref,
    own_ref,
    tab_ref,
):
    grid = levels * width
    chunk = 32
    row = lax.broadcasted_iota(jnp.int32, (LANES, LANES), 0)
    col = lax.broadcasted_iota(jnp.int32, (LANES, LANES), 1)
    even = (tile_ref[0, 0] & 1) == 0
    for side in range(2):
        flag = jnp.broadcast_to(flag_ref[0:1, side : side + 1], (LANES, LANES))
        source = jnp.where(flag > 0, LANES - 1 - col, col)
        turn = jnp.where(row == source, 1.0, 0.0)
        from_a = jnp.logical_xor(even, side == 0)
        place = slice(side * LANES, (side + 1) * LANES)
        turn_ref[0:LANES, place] = jnp.where(from_a, turn, 0.0).astype(BF16)
        turn_ref[LANES : 2 * LANES, place] = jnp.where(from_a, 0.0, turn).astype(BF16)
    entries = entry_ref.shape[0]
    tab_ref[...] = jnp.zeros_like(tab_ref)
    tab_ref[0:entries, :] = entry_ref[...].astype(F32)
    tab_ref[entries : entries + 1, :] = sun_ref[...].astype(F32)
    for i, part in enumerate(split3(mix_ref[...])):
        row = entries + 1 + i * (levels - 1)
        tab_ref[row : row + levels - 1, :] = part
    table_ref[...] = tab_ref[...].astype(BF16)
    shape = (grid, LANES)
    lane = lax.broadcasted_iota(jnp.int32, shape, 1)
    column = lax.broadcasted_iota(jnp.int32, shape, 0) % width
    faces = face_weights(cycle_ref[...])
    after = [jnp.where(column == width - 1, 0.0, pltpu.roll(w, grid - 1, 0)) for w in faces]
    across = cell_weights(faces, after)
    for k in range(7):
        weight_ref[k] = across[k]
    faces = face_weights(jnp.where(lane == 0, 0.0, edge_ref[...]))
    along = cell_weights(faces, [pltpu.roll(w, LANES - 1, 1) for w in faces])
    low3, low2, low1, here, high1, high2, high3 = along
    here = jnp.where(lane == 0, here + low1 + low2 + low3, here)
    low1 = jnp.where(lane == 1, low1 + low2 + low3, low1)
    low2 = jnp.where(lane == 2, low2 + low3, low2)
    here = jnp.where(lane == LANES - 1, here + high1 + high2 + high3, here)
    high1 = jnp.where(lane == LANES - 2, high1 + high2 + high3, high1)
    high2 = jnp.where(lane == LANES - 3, high2 + high3, high2)
    own_ref[0] = jnp.where(lane < 3, 0.0, low3)
    own_ref[1] = jnp.where(lane < 2, 0.0, low2)
    own_ref[2] = jnp.where(lane < 1, 0.0, low1)
    own_ref[3] = 1.0 + here + across[3]
    own_ref[4] = jnp.where(lane > LANES - 2, 0.0, high1)
    own_ref[5] = jnp.where(lane > LANES - 3, 0.0, high2)
    own_ref[6] = jnp.where(lane > LANES - 4, 0.0, high3)
    for level in range(levels):
        for start in range(0, quarter, chunk):
            cells = [
                x_ref[pl.ds(start * grid + level * width + col, chunk, stride=grid), :]
                for col in range(width)
            ]
            for col in range(width):
                cell = level * width + col
                total = cells[col] * own_ref[3, cell : cell + 1, :]
                for k in (-3, -2, -1, 1, 2, 3):
                    moved = pltpu.roll(cells[col], (-k) % LANES, 1)
                    total = total + moved * own_ref[3 + k, cell : cell + 1, :]
                    if 0 <= col + k < width:
                        total = total + cells[col + k] * weight_ref[3 + k, cell : cell + 1, :]
                base_ref[cell, start : start + chunk, :] = total


def maps_kernel(rank_ref, map_ref, off_ref, full_ref, last_ref, shift_ref, scratch_ref):
    rank = rank_ref[0, 0]
    count, quarter, species = full_ref.shape
    parts = species // quarter
    entries = count // parts
    row = lax.broadcasted_iota(jnp.int32, (species, species), 0)
    col = lax.broadcasted_iota(jnp.int32, (species, species), 1)
    shuffle = jnp.where(row == (col ^ (rank * quarter)), 1.0, 0.0).astype(BF16)
    for e in range(entries):
        moved = jnp.dot(map_ref[e], shuffle, preferred_element_type=F32).astype(BF16)
        for k in range(parts):
            scratch_ref[e * parts + k] = moved[k * quarter : (k + 1) * quarter, :]
    for e in range(entries):
        for k in range(parts):
            block = scratch_ref[e * parts + (rank ^ k)]
            full_ref[e * parts + k] = block
            if k < 2:
                last_ref[2 * e + k] = block
    for k in range(parts):
        shift_ref[k] = off_ref[rank ^ k]


def flow_kernel(
    levels,
    width,
    quarter,
    rank_ref,
    x_ref,
    base_ref,
    weight_ref,
    table_ref,
    turn_ref,
    a0_ref,
    a1_ref,
    b_ref,
    mine_ref,
    other_ref,
):
    grid = levels * width
    even = (rank_ref[0, 0] & 1) == 0
    halo = levels * 3 * quarter

    def received(begin, size):
        rows = slice(begin, begin + size)
        return jnp.concatenate([a0_ref[rows, :] + a1_ref[rows, :], b_ref[rows, :]], axis=1)

    def turned(values):
        both = jnp.dot(values, turn_ref[...], preferred_element_type=F32)
        return both[:, 0:LANES], both[:, LANES : 2 * LANES]

    _, split = turned(received(halo, 4 * levels))
    closing = split[0:levels] + split[levels : 2 * levels] + split[2 * levels : 3 * levels]
    closing = face_weights(closing)
    chunk = 32
    for level in range(levels):
        for start in range(0, quarter, chunk):
            begins = [(level * 3 + i) * quarter + start for i in range(3)]
            low, high = turned(
                jnp.concatenate([received(begin, chunk) for begin in begins], axis=0)
            )
            outer = {i - 3: low[i * chunk : (i + 1) * chunk] for i in range(3)}
            outer.update({width + i: high[i * chunk : (i + 1) * chunk] for i in range(3)})
            moved = []
            for c in range(width):
                cell = level * width + c
                total = base_ref[cell, start : start + chunk, :]
                for k in range(-3, 4):
                    if c + k in outer and not (c == width - 1 and k == 3):
                        total = total + outer[c + k] * weight_ref[3 + k, cell : cell + 1, :]
                if c == width - 1:
                    for k in range(-3, 3):
                        if width + k in outer:
                            value = outer[width + k]
                        else:
                            begin = start * grid + level * width + width + k
                            value = x_ref[pl.ds(begin, chunk, stride=grid), :]
                        total = total - value * closing[3 + k][level : level + 1, :]
                moved.append(total)
            for k in range(width // 2):
                low, high = moved[k], moved[width // 2 + k]
                begin = (level * (width // 2) + k) * quarter + start
                mine_ref[begin : begin + chunk, :] = jnp.where(even, low, high).astype(BF16)
                other_ref[begin : begin + chunk, :] = jnp.where(even, high, low).astype(BF16)
    begin = grid // 2 * quarter
    mine_ref[begin : begin + TABLE_ROWS, :] = table_ref[...]
    other_ref[begin : begin + TABLE_ROWS, :] = table_ref[...]


def tables_of(rank, tails):
    lane = lax.broadcasted_iota(jnp.int32, (TABLE_ROWS, LANES), 1)
    t0, t1, t2, t3 = [t.astype(F32) for t in tails]
    odd = (rank & 1) > 0
    t0, t1 = jnp.where(odd, t1, t0), jnp.where(odd, t0, t1)
    t2, t3 = jnp.where(odd, t3, t2), jnp.where(odd, t2, t3)
    upper = (rank & 2) > 0
    t0, t2 = jnp.where(upper, t2, t0), jnp.where(upper, t0, t2)
    t1, t3 = jnp.where(upper, t3, t1), jnp.where(upper, t1, t3)
    return block_transpose((t0, t1, t2, t3), lane)


def chem_kernel(
    levels,
    width,
    quarter,
    entries,
    substeps,
    rank_ref,
    block0_ref,
    block1_ref,
    block2_ref,
    block3_ref,
    tail0_ref,
    tail1_ref,
    tail2_ref,
    tail3_ref,
    map_ref,
    last_ref,
    off_ref,
    keep_ref,
    give_ref,
    chem_ref,
):
    block_refs = (block0_ref, block1_ref, block2_ref, block3_ref)
    tail_refs = (tail0_ref, tail1_ref, tail2_ref, tail3_ref)
    parts = len(block_refs)
    species = parts * quarter
    half = width // 2
    even = (rank_ref[0, 0] & 1) == 0
    tables = tables_of(rank_ref[0, 0], [r[...] for r in tail_refs])
    columns = [jnp.where(even, tables[k], tables[half + k]) for k in range(half)]

    def row_of(index):
        return jnp.concatenate([columns[k][index : index + 1, :] for k in range(half)], axis=1)

    def block(part, group):
        return block_refs[part][group * quarter : (group + 1) * quarter, :]

    sun = substeps * levels
    lit = row_of(sun) > 0.0
    any_lit = jnp.max(row_of(sun)) > 0.0

    @pl.when(any_lit)
    def lit_tile():
        start = []
        for level in range(levels):
            cells = [
                jnp.concatenate([block(p, level * half + k) for p in range(parts)], axis=0)
                for k in range(half)
            ]
            start.append(jnp.concatenate(cells, axis=1))
        state = list(start)
        for step in range(substeps):
            final = step == substeps - 1
            rows = 2 * quarter if final else species
            matrix = last_ref[...] if final else map_ref[...]
            for level in range(levels):
                product = jnp.dot(matrix, state[level], preferred_element_type=F32)
                entry = row_of(step * levels + level)
                chosen = product[0:rows] + off_ref[0:rows, 0:1]
                for e in range(1, entries):
                    chosen = jnp.where(
                        entry == float(e),
                        product[e * rows : (e + 1) * rows] + off_ref[0:rows, e : e + 1],
                        chosen,
                    )
                chosen = jnp.maximum(chosen, 0.0)
                if not final:
                    state[level] = chosen.astype(BF16)
                    continue
                chem = jnp.where(lit, chosen, start[level][0:rows].astype(F32))
                for k in range(half):
                    chem_ref[level * half + k] = chem[:, k * LANES : (k + 1) * LANES]

    @pl.when(jnp.logical_not(any_lit))
    def dark_tile():
        for group in range(levels * half):
            for p in range(2):
                rows = slice(p * quarter, (p + 1) * quarter)
                chem_ref[group, rows, :] = block(p, group).astype(F32)

    chunk = 32
    for k in range(half):
        pieces = [
            columns[k][sun + 1 + i * (levels - 1) : sun + 1 + (i + 1) * (levels - 1), :]
            for i in range(3)
        ]
        mixed = pieces[0] + pieces[1] + pieces[2]
        mixing = [mixed[i : i + 1, :] for i in range(levels - 1)]
        inverse, ratio = [], []
        for level in range(levels):
            diagonal = 1.0
            if level > 0:
                diagonal = diagonal + mixing[level - 1]
            if level < levels - 1:
                diagonal = diagonal + mixing[level]
            if level > 0:
                diagonal = diagonal - mixing[level - 1] * ratio[level - 1]
            inverse.append(1.0 / diagonal)
            if level < levels - 1:
                ratio.append(mixing[level] * inverse[level])
        for p, out_ref in enumerate((keep_ref, give_ref)):
            for begin in range(0, quarter, chunk):
                solved = []
                for level in range(levels):
                    rows = slice(p * quarter + begin, p * quarter + begin + chunk)
                    value = chem_ref[level * half + k, rows, :]
                    if level > 0:
                        value = value + mixing[level - 1] * solved[-1]
                    solved.append(value * inverse[level])
                for level in range(levels - 2, -1, -1):
                    solved[level] = solved[level] + ratio[level] * solved[level + 1]
                for level in range(levels):
                    place = begin * levels * half + level * half + k
                    out_ref[pl.ds(place, chunk, stride=levels * half), :] = solved[level]


def keep_kernel(rank_ref, keep_ref, out_hbm, sem):
    copy = pltpu.make_async_copy(keep_ref, out_hbm.at[:, rank_ref[0, 0] & 1], sem)
    copy.start()
    copy.wait()


def fill_kernel(rank_ref, got_ref, part_hbm, out_hbm, sem):
    del part_hbm
    copy = pltpu.make_async_copy(got_ref, out_hbm.at[:, 1 - (rank_ref[0, 0] & 1)], sem)
    copy.start()
    copy.wait()


def shards(
    tracers,
    courant_cycle,
    courant_edge,
    seam_flags,
    sunlit,
    table_entry,
    linear_maps,
    offsets,
    mixing,
):
    quarter, levels, width, length = tracers.shape
    grid = levels * width
    substeps = table_entry.shape[0]
    entries, species, _ = linear_maps.shape
    count = lax.axis_size("tile")
    parts = lax.axis_size("trc")
    pairs = [(i, i ^ 1) for i in range(count)]
    seams = [(i, (i + (1 if i % 2 else -1)) % count) for i in range(count)]
    tile = lax.axis_index("tile").astype(jnp.int32).reshape(1, 1)
    halo = levels * 3 * quarter
    pieces = 4
    shape = jax.ShapeDtypeStruct
    brought = [
        tracers.reshape(quarter * grid, length),
        courant_cycle.reshape(grid, length),
        courant_edge.reshape(grid, length),
        table_entry,
        sunlit,
        mixing,
        seam_flags,
    ]
    to_a, to_b, x, cycle, edge, entry, sun, mix, flags = pl.pallas_call(
        functools.partial(pack_kernel, levels, width, quarter, pieces),
        out_shape=(
            shape((halo + 4 * levels, length), BF16),
            shape((halo + 4 * levels, length), BF16),
            *[shape(array.shape, array.dtype) for array in brought],
        ),
        in_specs=[smem()] + [hbm()] * len(brought),
        out_specs=(vmem(),) * (2 + len(brought)),
        scratch_shapes=[pltpu.SemaphoreType.DMA((pieces + len(brought) - 1,))],
        compiler_params=params(8),
        name="pack",
    )(tile, *[in_hbm(array) for array in brought])
    from_a0 = lax.ppermute(to_a, "tile", pairs[:2])
    from_b = lax.ppermute(to_b, "tile", seams)
    from_a1 = lax.ppermute(to_a, "tile", pairs[2:])
    rank = lax.axis_index("trc").astype(jnp.int32).reshape(1, 1)
    base, weights, table, turns = pl.pallas_call(
        functools.partial(local_kernel, levels, width, quarter),
        out_shape=(
            shape((grid, quarter, length), F32),
            shape((7, grid, length), F32),
            shape((TABLE_ROWS, length), BF16),
            shape((2 * length, 2 * length), BF16),
        ),
        in_specs=[smem()] + [vmem()] * 7,
        out_specs=(vmem(),) * 4,
        scratch_shapes=[
            pltpu.VMEM((7, grid, length), F32),
            pltpu.VMEM((TABLE_ROWS, length), F32),
        ],
        compiler_params=params(8),
        cost_estimate=pl.CostEstimate(flops=4000000, bytes_accessed=1 << 20, transcendentals=0),
        name="local",
    )(
        tile,
        flags,
        x,
        cycle,
        edge,
        entry.reshape(substeps * levels, length),
        sun.reshape(1, length),
        mix.reshape(levels - 1, length),
    )
    rows = grid // 2 * quarter
    mine, other = pl.pallas_call(
        functools.partial(flow_kernel, levels, width, quarter),
        out_shape=(shape((rows + TABLE_ROWS, length), BF16),) * 2,
        in_specs=[smem()] + [vmem()] * 8,
        out_specs=(vmem(),) * 2,
        compiler_params=params(8),
        name="flow",
    )(rank, x, base, weights, table, turns, from_a0, from_a1, from_b)
    swap = {k: [(i, i ^ k) for i in range(parts)] for k in (1, 2, 3)}
    second = lax.ppermute(mine, "trc", swap[2])
    third = lax.ppermute(other, "trc", swap[3])
    first = lax.ppermute(other, "trc", swap[1])
    full, last, shift = pl.pallas_call(
        maps_kernel,
        out_shape=(
            shape((entries * parts, quarter, species), BF16),
            shape((2 * entries, quarter, species), BF16),
            shape((parts, quarter, entries), F32),
        ),
        in_specs=[smem()] + [vmem()] * 2,
        out_specs=(vmem(),) * 3,
        scratch_shapes=[pltpu.VMEM((entries * parts, quarter, species), BF16)],
        compiler_params=params(8),
        cost_estimate=pl.CostEstimate(flops=4000000, bytes_accessed=1 << 20, transcendentals=0),
        name="maps",
    )(rank, linear_maps, offsets.T.reshape(parts, quarter, entries))
    blocks = [mine, first, second, third]
    keep, give = pl.pallas_call(
        functools.partial(chem_kernel, levels, width, quarter, entries, substeps),
        out_shape=(shape((rows, length), F32),) * 2,
        in_specs=[smem()] + [vmem()] * 11,
        out_specs=(vmem(),) * 2,
        scratch_shapes=[pltpu.VMEM((grid // 2, 2 * quarter, length), F32)],
        compiler_params=params(24),
        name="chem",
    )(
        rank,
        *blocks,
        *[b[rows:] for b in blocks],
        full.reshape(entries * species, species),
        last.reshape(2 * entries * quarter, species),
        shift.reshape(species, entries),
    )
    got = lax.ppermute(give, "trc", swap[1])
    pair = (quarter * levels, width // 2, length)
    whole = shape((quarter * levels, 2, width // 2, length), F32)
    part = pl.pallas_call(
        keep_kernel,
        out_shape=whole,
        in_specs=[smem(), vmem()],
        out_specs=hbm(),
        scratch_shapes=[pltpu.SemaphoreType.DMA],
        compiler_params=params(4),
        cost_estimate=pl.CostEstimate(flops=1000000, bytes_accessed=1 << 19, transcendentals=0),
        name="keep",
    )(rank, keep.reshape(pair))
    out = pl.pallas_call(
        fill_kernel,
        out_shape=whole,
        in_specs=[smem(), vmem(), hbm()],
        out_specs=hbm(),
        scratch_shapes=[pltpu.SemaphoreType.DMA],
        input_output_aliases={2: 0},
        compiler_params=params(4),
        name="fill",
    )(rank, got.reshape(pair), part)
    return out.reshape(quarter, levels, width, length)


def solution(mesh):
    placed = (
        P("trc", None, "tile", None),
        P(None, "tile", None),
        P(None, "tile", None),
        P("tile", None),
        P("tile", "trc"),
        P(None, None, "tile", "trc"),
        P(),
        P(),
        P(None, "tile", "trc"),
    )
    return jax.shard_map(
        shards, mesh=mesh, in_specs=placed, out_specs=P("trc", None, "tile", None), check_vma=False
    )
```

```python
import functools

import jax
import jax.numpy as jnp
from jax import lax
from jax.experimental import pallas as pl
from jax.experimental.pallas import tpu as pltpu
from jax.sharding import PartitionSpec as P

F32 = jnp.float32
BF16 = jnp.bfloat16
LANES = 128
TABLE_ROWS = 32


def vmem():
    return pl.BlockSpec(memory_space=pltpu.VMEM)


def smem():
    return pl.BlockSpec(memory_space=pltpu.SMEM)


def hbm():
    return pl.BlockSpec(memory_space=pltpu.HBM)


def in_hbm(array):
    return pltpu.with_memory_space_constraint(array, pltpu.HBM)


def params(mib):
    return pltpu.CompilerParams(vmem_limit_bytes=mib << 20)


def face_weights(courant):
    speed = jnp.abs(courant)
    rest = 1.0 - speed
    mid = courant * rest * rest
    far = -courant * speed * rest
    centre = courant * speed * (3.0 - 2.0 * speed)
    positive = courant > 0.0
    far_low = jnp.where(positive, far, 0.0)
    far_high = far - far_low
    centre_low = jnp.where(positive, centre, 0.0)
    centre_high = centre - centre_low
    small, large = 1.0 / 12.0, 7.0 / 12.0
    return [
        -small * far_low,
        large * far_low - small * mid,
        large * (mid + far_low) - small * far_high + centre_low,
        large * (mid + far_high) - small * far_low + centre_high,
        large * far_high - small * mid,
        -small * far_high,
    ]


def cell_weights(before, after):
    zero = jnp.zeros_like(before[0])
    return [a - b for a, b in zip(before + [zero], [zero] + after)]


def block_transpose(rows, lane):
    low = lane < 64
    even = (lane & 32) == 0
    r0, r1, r2, r3 = rows
    b0 = jnp.where(low, r0, pltpu.roll(r2, 64, 1))
    b2 = jnp.where(low, pltpu.roll(r0, 64, 1), r2)
    b1 = jnp.where(low, r1, pltpu.roll(r3, 64, 1))
    b3 = jnp.where(low, pltpu.roll(r1, 64, 1), r3)
    return (
        jnp.where(even, b0, pltpu.roll(b1, 32, 1)),
        jnp.where(even, pltpu.roll(b0, 96, 1), b1),
        jnp.where(even, b2, pltpu.roll(b3, 32, 1)),
        jnp.where(even, pltpu.roll(b2, 96, 1), b3),
    )


def split3(values):
    high = values.astype(BF16).astype(F32)
    rest = values - high
    mid = rest.astype(BF16).astype(F32)
    return high, mid, rest - mid


def pack_kernel(levels, width, quarter, pieces, *refs):
    even = (refs[0][0, 0] & 1) == 0
    refs = refs[1:]
    count = (len(refs) - 3) // 2
    sources, (a_ref, b_ref), targets = refs[:count], refs[count : count + 2], refs[count + 2 : -1]
    sems = refs[-1]
    x_ref, u_ref = targets[0], targets[1]
    grid = levels * width
    part = quarter // pieces
    small, large = [], []
    for i in range(1, count):
        small.append(pltpu.make_async_copy(sources[i], targets[i], sems.at[pieces + i - 1]))
    for i in range(pieces):
        rows = pl.ds(i * part * grid, part * grid)
        large.append(pltpu.make_async_copy(sources[0].at[rows], x_ref.at[rows], sems.at[i]))
    small[0].start()
    for copy in large + small[1:]:
        copy.start()
    small[0].wait()
    row = levels * 3 * quarter
    parts = split3(u_ref[pl.ds(0, levels, stride=width), :])
    parts = jnp.concatenate(parts + (jnp.zeros_like(parts[0]),), axis=0)
    a_ref[row : row + 4 * levels, :] = parts.astype(BF16)
    b_ref[row : row + 4 * levels, :] = parts.astype(BF16)
    for i in range(pieces):
        large[i].wait()
        for level in range(levels):
            start = i * part * grid + level * width
            cells = [x_ref[pl.ds(start + c, part, stride=grid), :] for c in range(width)]
            for c in range(3):
                row = (level * 3 + c) * quarter + i * part
                low, high = cells[c], cells[width - 3 + c]
                a_ref[row : row + part, :] = jnp.where(even, high, low).astype(BF16)
                b_ref[row : row + part, :] = jnp.where(even, low, high).astype(BF16)
    for copy in small[1:]:
        copy.wait()


def local_kernel(
    levels,
    width,
    quarter,
    flag_ref,
    x_ref,
    cycle_ref,
    edge_ref,
    entry_ref,
    sun_ref,
    mix_ref,
    base_ref,
    weight_ref,
    table_ref,
    turn_ref,
    own_ref,
    tab_ref,
):
    grid = levels * width
    chunk = 32
    row = lax.broadcasted_iota(jnp.int32, (LANES, LANES), 0)
    col = lax.broadcasted_iota(jnp.int32, (LANES, LANES), 1)
    for side in range(2):
        flag = jnp.broadcast_to(flag_ref[0:1, side : side + 1], (LANES, LANES))
        source = jnp.where(flag > 0, LANES - 1 - col, col)
        turn_ref[side] = jnp.where(row == source, 1.0, 0.0).astype(BF16)
    entries = entry_ref.shape[0]
    tab_ref[...] = jnp.zeros_like(tab_ref)
    tab_ref[0:entries, :] = entry_ref[...].astype(F32)
    tab_ref[entries : entries + 1, :] = sun_ref[...].astype(F32)
    for i, part in enumerate(split3(mix_ref[...])):
        row = entries + 1 + i * (levels - 1)
        tab_ref[row : row + levels - 1, :] = part
    table_ref[...] = tab_ref[...].astype(BF16)
    shape = (grid, LANES)
    lane = lax.broadcasted_iota(jnp.int32, shape, 1)
    column = lax.broadcasted_iota(jnp.int32, shape, 0) % width
    faces = face_weights(cycle_ref[...])
    after = [jnp.where(column == width - 1, 0.0, pltpu.roll(w, grid - 1, 0)) for w in faces]
    across = cell_weights(faces, after)
    for k in range(7):
        weight_ref[k] = across[k]
    faces = face_weights(jnp.where(lane == 0, 0.0, edge_ref[...]))
    along = cell_weights(faces, [pltpu.roll(w, LANES - 1, 1) for w in faces])
    low3, low2, low1, here, high1, high2, high3 = along
    here = jnp.where(lane == 0, here + low1 + low2 + low3, here)
    low1 = jnp.where(lane == 1, low1 + low2 + low3, low1)
    low2 = jnp.where(lane == 2, low2 + low3, low2)
    here = jnp.where(lane == LANES - 1, here + high1 + high2 + high3, here)
    high1 = jnp.where(lane == LANES - 2, high1 + high2 + high3, high1)
    high2 = jnp.where(lane == LANES - 3, high2 + high3, high2)
    own_ref[0] = jnp.where(lane < 3, 0.0, low3)
    own_ref[1] = jnp.where(lane < 2, 0.0, low2)
    own_ref[2] = jnp.where(lane < 1, 0.0, low1)
    own_ref[3] = 1.0 + here + across[3]
    own_ref[4] = jnp.where(lane > LANES - 2, 0.0, high1)
    own_ref[5] = jnp.where(lane > LANES - 3, 0.0, high2)
    own_ref[6] = jnp.where(lane > LANES - 4, 0.0, high3)
    for level in range(levels):
        for start in range(0, quarter, chunk):
            cells = [
                x_ref[pl.ds(start * grid + level * width + col, chunk, stride=grid), :]
                for col in range(width)
            ]
            for col in range(width):
                cell = level * width + col
                total = cells[col] * own_ref[3, cell : cell + 1, :]
                for k in (-3, -2, -1, 1, 2, 3):
                    moved = pltpu.roll(cells[col], (-k) % LANES, 1)
                    total = total + moved * own_ref[3 + k, cell : cell + 1, :]
                    if 0 <= col + k < width:
                        total = total + cells[col + k] * weight_ref[3 + k, cell : cell + 1, :]
                base_ref[cell, start : start + chunk, :] = total


def maps_kernel(rank_ref, map_ref, off_ref, full_ref, last_ref, shift_ref, scratch_ref):
    rank = rank_ref[0, 0]
    count, quarter, species = full_ref.shape
    parts = species // quarter
    entries = count // parts
    row = lax.broadcasted_iota(jnp.int32, (species, species), 0)
    col = lax.broadcasted_iota(jnp.int32, (species, species), 1)
    shuffle = jnp.where(row == (col ^ (rank * quarter)), 1.0, 0.0).astype(BF16)
    for e in range(entries):
        moved = jnp.dot(map_ref[e], shuffle, preferred_element_type=F32).astype(BF16)
        for k in range(parts):
            scratch_ref[e * parts + k] = moved[k * quarter : (k + 1) * quarter, :]
    for e in range(entries):
        for k in range(parts):
            block = scratch_ref[e * parts + (rank ^ k)]
            full_ref[e * parts + k] = block
            if k < 2:
                last_ref[2 * e + k] = block
    for k in range(parts):
        shift_ref[k] = off_ref[rank ^ k]


def halo_terms(levels, width, quarter, side, level, start, chunk, closing, x_ref, weight_ref, turn_ref, halo_of):
    grid = levels * width
    begins = [(level * 3 + i) * quarter + start for i in range(3)]
    values = jnp.concatenate([halo_of(begin, chunk) for begin in begins], axis=0)
    values = jnp.dot(values, turn_ref[side], preferred_element_type=F32)
    offset = width if side else -3
    outer = {offset + i: values[i * chunk : (i + 1) * chunk] for i in range(3)}
    terms = []
    for c in range(width):
        cell = level * width + c
        total = None
        for k in range(-3, 4):
            if c + k in outer and not (c == width - 1 and k == 3):
                term = outer[c + k] * weight_ref[3 + k, cell : cell + 1, :]
                total = term if total is None else total + term
        if side and c == width - 1:
            for k in range(-3, 3):
                if width + k in outer:
                    value = outer[width + k]
                else:
                    begin = start * grid + level * width + width + k
                    value = x_ref[pl.ds(begin, chunk, stride=grid), :]
                total = total - value * closing[3 + k][level : level + 1, :]
        terms.append(total)
    return terms


def closing_weights(levels, quarter, turn_ref, halo_of):
    split = halo_of(levels * 3 * quarter, 4 * levels)
    split = jnp.dot(split, turn_ref[1], preferred_element_type=F32)
    return face_weights(split[0:levels] + split[levels : 2 * levels] + split[2 * levels : 3 * levels])


def near_kernel(
    levels, width, quarter, tile_ref, x_ref, base_ref, weight_ref, turn_ref, a0_ref, a1_ref, near_ref
):
    chunk = 32
    even = (tile_ref[0, 0] & 1) == 0

    def halo_of(begin, size):
        return a0_ref[begin : begin + size, :] + a1_ref[begin : begin + size, :]

    def work(side):
        closing = closing_weights(levels, quarter, turn_ref, halo_of) if side else None
        for level in range(levels):
            for start in range(0, quarter, chunk):
                terms = halo_terms(
                    levels, width, quarter, side, level, start, chunk, closing,
                    x_ref, weight_ref, turn_ref, halo_of,
                )
                for c in range(width):
                    cell = level * width + c
                    total = base_ref[cell, start : start + chunk, :]
                    if terms[c] is not None:
                        total = total + terms[c]
                    near_ref[cell, start : start + chunk, :] = total

    pl.when(even)(lambda: work(1))
    pl.when(jnp.logical_not(even))(lambda: work(0))


def flow_kernel(
    levels,
    width,
    quarter,
    rank_ref,
    tile_ref,
    x_ref,
    near_ref,
    weight_ref,
    table_ref,
    turn_ref,
    b_ref,
    mine_ref,
    other_ref,
):
    chunk = 32
    half = width // 2
    first_core = (rank_ref[0, 0] & 1) == 0
    even = (tile_ref[0, 0] & 1) == 0

    def halo_of(begin, size):
        return b_ref[begin : begin + size, :]

    def work(side):
        closing = closing_weights(levels, quarter, turn_ref, halo_of) if side else None
        for level in range(levels):
            for start in range(0, quarter, chunk):
                terms = halo_terms(
                    levels, width, quarter, side, level, start, chunk, closing,
                    x_ref, weight_ref, turn_ref, halo_of,
                )
                moved = []
                for c in range(width):
                    total = near_ref[level * width + c, start : start + chunk, :]
                    moved.append(total if terms[c] is None else total + terms[c])
                for k in range(half):
                    low, high = moved[k], moved[half + k]
                    begin = (level * half + k) * quarter + start
                    mine_ref[begin : begin + chunk, :] = jnp.where(first_core, low, high).astype(BF16)
                    other_ref[begin : begin + chunk, :] = jnp.where(first_core, high, low).astype(BF16)

    pl.when(even)(lambda: work(0))
    pl.when(jnp.logical_not(even))(lambda: work(1))
    begin = levels * half * quarter
    mine_ref[begin : begin + TABLE_ROWS, :] = table_ref[...]
    other_ref[begin : begin + TABLE_ROWS, :] = table_ref[...]


def tables_of(rank, tails):
    lane = lax.broadcasted_iota(jnp.int32, (TABLE_ROWS, LANES), 1)
    t0, t1, t2, t3 = [t.astype(F32) for t in tails]
    odd = (rank & 1) > 0
    t0, t1 = jnp.where(odd, t1, t0), jnp.where(odd, t0, t1)
    t2, t3 = jnp.where(odd, t3, t2), jnp.where(odd, t2, t3)
    upper = (rank & 2) > 0
    t0, t2 = jnp.where(upper, t2, t0), jnp.where(upper, t0, t2)
    t1, t3 = jnp.where(upper, t3, t1), jnp.where(upper, t1, t3)
    return block_transpose((t0, t1, t2, t3), lane)


def chem_kernel(
    levels,
    width,
    quarter,
    entries,
    substeps,
    rank_ref,
    block0_ref,
    block1_ref,
    block2_ref,
    block3_ref,
    tail0_ref,
    tail1_ref,
    tail2_ref,
    tail3_ref,
    map_ref,
    last_ref,
    off_ref,
    keep_ref,
    give_ref,
    chem_ref,
):
    block_refs = (block0_ref, block1_ref, block2_ref, block3_ref)
    tail_refs = (tail0_ref, tail1_ref, tail2_ref, tail3_ref)
    parts = len(block_refs)
    species = parts * quarter
    half = width // 2
    even = (rank_ref[0, 0] & 1) == 0
    tables = tables_of(rank_ref[0, 0], [r[...] for r in tail_refs])
    columns = [jnp.where(even, tables[k], tables[half + k]) for k in range(half)]

    def row_of(index):
        return jnp.concatenate([columns[k][index : index + 1, :] for k in range(half)], axis=1)

    def block(part, group):
        return block_refs[part][group * quarter : (group + 1) * quarter, :]

    sun = substeps * levels
    lit = row_of(sun) > 0.0
    any_lit = jnp.max(row_of(sun)) > 0.0

    @pl.when(any_lit)
    def lit_tile():
        start = []
        for level in range(levels):
            cells = [
                jnp.concatenate([block(p, level * half + k) for p in range(parts)], axis=0)
                for k in range(half)
            ]
            start.append(jnp.concatenate(cells, axis=1))
        state = list(start)
        for step in range(substeps):
            final = step == substeps - 1
            rows = 2 * quarter if final else species
            matrix = last_ref[...] if final else map_ref[...]
            for level in range(levels):
                product = jnp.dot(matrix, state[level], preferred_element_type=F32)
                entry = row_of(step * levels + level)
                chosen = product[0:rows] + off_ref[0:rows, 0:1]
                for e in range(1, entries):
                    chosen = jnp.where(
                        entry == float(e),
                        product[e * rows : (e + 1) * rows] + off_ref[0:rows, e : e + 1],
                        chosen,
                    )
                chosen = jnp.maximum(chosen, 0.0)
                if not final:
                    state[level] = chosen.astype(BF16)
                    continue
                chem = jnp.where(lit, chosen, start[level][0:rows].astype(F32))
                for k in range(half):
                    chem_ref[level * half + k] = chem[:, k * LANES : (k + 1) * LANES]

    @pl.when(jnp.logical_not(any_lit))
    def dark_tile():
        for group in range(levels * half):
            for p in range(2):
                rows = slice(p * quarter, (p + 1) * quarter)
                chem_ref[group, rows, :] = block(p, group).astype(F32)

    chunk = 32
    for k in range(half):
        pieces = [
            columns[k][sun + 1 + i * (levels - 1) : sun + 1 + (i + 1) * (levels - 1), :]
            for i in range(3)
        ]
        mixed = pieces[0] + pieces[1] + pieces[2]
        mixing = [mixed[i : i + 1, :] for i in range(levels - 1)]
        inverse, ratio = [], []
        for level in range(levels):
            diagonal = 1.0
            if level > 0:
                diagonal = diagonal + mixing[level - 1]
            if level < levels - 1:
                diagonal = diagonal + mixing[level]
            if level > 0:
                diagonal = diagonal - mixing[level - 1] * ratio[level - 1]
            inverse.append(1.0 / diagonal)
            if level < levels - 1:
                ratio.append(mixing[level] * inverse[level])
        for p, out_ref in enumerate((keep_ref, give_ref)):
            for begin in range(0, quarter, chunk):
                solved = []
                for level in range(levels):
                    rows = slice(p * quarter + begin, p * quarter + begin + chunk)
                    value = chem_ref[level * half + k, rows, :]
                    if level > 0:
                        value = value + mixing[level - 1] * solved[-1]
                    solved.append(value * inverse[level])
                for level in range(levels - 2, -1, -1):
                    solved[level] = solved[level] + ratio[level] * solved[level + 1]
                for level in range(levels):
                    place = begin * levels * half + level * half + k
                    out_ref[pl.ds(place, chunk, stride=levels * half), :] = solved[level]


def keep_kernel(rank_ref, keep_ref, out_hbm, sem):
    copy = pltpu.make_async_copy(keep_ref, out_hbm.at[:, rank_ref[0, 0] & 1], sem)
    copy.start()
    copy.wait()


def fill_kernel(rank_ref, got_ref, part_hbm, out_hbm, sem):
    del part_hbm
    copy = pltpu.make_async_copy(got_ref, out_hbm.at[:, 1 - (rank_ref[0, 0] & 1)], sem)
    copy.start()
    copy.wait()


def shards(
    tracers,
    courant_cycle,
    courant_edge,
    seam_flags,
    sunlit,
    table_entry,
    linear_maps,
    offsets,
    mixing,
):
    quarter, levels, width, length = tracers.shape
    grid = levels * width
    substeps = table_entry.shape[0]
    entries, species, _ = linear_maps.shape
    count = lax.axis_size("tile")
    parts = lax.axis_size("trc")
    pairs = [(i, i ^ 1) for i in range(count)]
    seams = [(i, (i + (1 if i % 2 else -1)) % count) for i in range(count)]
    tile = lax.axis_index("tile").astype(jnp.int32).reshape(1, 1)
    halo = levels * 3 * quarter
    pieces = 4
    shape = jax.ShapeDtypeStruct
    brought = [
        tracers.reshape(quarter * grid, length),
        courant_cycle.reshape(grid, length),
        courant_edge.reshape(grid, length),
        table_entry,
        sunlit,
        mixing,
        seam_flags,
    ]
    to_a, to_b, x, cycle, edge, entry, sun, mix, flags = pl.pallas_call(
        functools.partial(pack_kernel, levels, width, quarter, pieces),
        out_shape=(
            shape((halo + 4 * levels, length), BF16),
            shape((halo + 4 * levels, length), BF16),
            *[shape(array.shape, array.dtype) for array in brought],
        ),
        in_specs=[smem()] + [hbm()] * len(brought),
        out_specs=(vmem(),) * (2 + len(brought)),
        scratch_shapes=[pltpu.SemaphoreType.DMA((pieces + len(brought) - 1,))],
        compiler_params=params(8),
        name="pack",
    )(tile, *[in_hbm(array) for array in brought])
    from_a0 = lax.ppermute(to_a, "tile", pairs[:2])
    from_b = lax.ppermute(to_b, "tile", seams)
    from_a1 = lax.ppermute(to_a, "tile", pairs[2:])
    rank = lax.axis_index("trc").astype(jnp.int32).reshape(1, 1)
    base, weights, table, turns = pl.pallas_call(
        functools.partial(local_kernel, levels, width, quarter),
        out_shape=(
            shape((grid, quarter, length), F32),
            shape((7, grid, length), F32),
            shape((TABLE_ROWS, length), BF16),
            shape((2, length, length), BF16),
        ),
        in_specs=[vmem()] * 7,
        out_specs=(vmem(),) * 4,
        scratch_shapes=[
            pltpu.VMEM((7, grid, length), F32),
            pltpu.VMEM((TABLE_ROWS, length), F32),
        ],
        compiler_params=params(8),
        cost_estimate=pl.CostEstimate(flops=4000000, bytes_accessed=1 << 20, transcendentals=0),
        name="local",
    )(
        flags,
        x,
        cycle,
        edge,
        entry.reshape(substeps * levels, length),
        sun.reshape(1, length),
        mix.reshape(levels - 1, length),
    )
    rows = grid // 2 * quarter
    near = pl.pallas_call(
        functools.partial(near_kernel, levels, width, quarter),
        out_shape=shape((grid, quarter, length), F32),
        in_specs=[smem()] + [vmem()] * 6,
        out_specs=vmem(),
        compiler_params=params(8),
        name="near",
    )(tile, x, base, weights, turns, from_a0, from_a1)
    mine, other = pl.pallas_call(
        functools.partial(flow_kernel, levels, width, quarter),
        out_shape=(shape((rows + TABLE_ROWS, length), BF16),) * 2,
        in_specs=[smem()] * 2 + [vmem()] * 6,
        out_specs=(vmem(),) * 2,
        compiler_params=params(8),
        name="flow",
    )(rank, tile, x, near, weights, table, turns, from_b)
    swap = {k: [(i, i ^ k) for i in range(parts)] for k in (1, 2, 3)}
    second = lax.ppermute(mine, "trc", swap[2])
    third = lax.ppermute(other, "trc", swap[3])
    first = lax.ppermute(other, "trc", swap[1])
    full, last, shift = pl.pallas_call(
        maps_kernel,
        out_shape=(
            shape((entries * parts, quarter, species), BF16),
            shape((2 * entries, quarter, species), BF16),
            shape((parts, quarter, entries), F32),
        ),
        in_specs=[smem()] + [vmem()] * 2,
        out_specs=(vmem(),) * 3,
        scratch_shapes=[pltpu.VMEM((entries * parts, quarter, species), BF16)],
        compiler_params=params(8),
        cost_estimate=pl.CostEstimate(flops=4000000, bytes_accessed=1 << 20, transcendentals=0),
        name="maps",
    )(rank, linear_maps, offsets.T.reshape(parts, quarter, entries))
    blocks = [mine, first, second, third]
    keep, give = pl.pallas_call(
        functools.partial(chem_kernel, levels, width, quarter, entries, substeps),
        out_shape=(shape((rows, length), F32),) * 2,
        in_specs=[smem()] + [vmem()] * 11,
        out_specs=(vmem(),) * 2,
        scratch_shapes=[pltpu.VMEM((grid // 2, 2 * quarter, length), F32)],
        compiler_params=params(24),
        name="chem",
    )(
        rank,
        *blocks,
        *[b[rows:] for b in blocks],
        full.reshape(entries * species, species),
        last.reshape(2 * entries * quarter, species),
        shift.reshape(species, entries),
    )
    got = lax.ppermute(give, "trc", swap[1])
    pair = (quarter * levels, width // 2, length)
    whole = shape((quarter * levels, 2, width // 2, length), F32)
    part = pl.pallas_call(
        keep_kernel,
        out_shape=whole,
        in_specs=[smem(), vmem()],
        out_specs=hbm(),
        scratch_shapes=[pltpu.SemaphoreType.DMA],
        compiler_params=params(4),
        cost_estimate=pl.CostEstimate(flops=1000000, bytes_accessed=1 << 19, transcendentals=0),
        name="keep",
    )(rank, keep.reshape(pair))
    out = pl.pallas_call(
        fill_kernel,
        out_shape=whole,
        in_specs=[smem(), vmem(), hbm()],
        out_specs=hbm(),
        scratch_shapes=[pltpu.SemaphoreType.DMA],
        input_output_aliases={2: 0},
        compiler_params=params(4),
        name="fill",
    )(rank, got.reshape(pair), part)
    return out.reshape(quarter, levels, width, length)


def solution(mesh):
    placed = (
        P("trc", None, "tile", None),
        P(None, "tile", None),
        P(None, "tile", None),
        P("tile", None),
        P("tile", "trc"),
        P(None, None, "tile", "trc"),
        P(),
        P(),
        P(None, "tile", "trc"),
    )
    return jax.shard_map(
        shards, mesh=mesh, in_specs=placed, out_specs=P("trc", None, "tile", None), check_vma=False
    )
```

```python
import functools

import jax
import jax.numpy as jnp
from jax import lax
from jax.experimental import pallas as pl
from jax.experimental.pallas import tpu as pltpu
from jax.sharding import PartitionSpec as P

F32 = jnp.float32
BF16 = jnp.bfloat16
LANES = 128
TABLE_ROWS = 32


def vmem():
    return pl.BlockSpec(memory_space=pltpu.VMEM)


def smem():
    return pl.BlockSpec(memory_space=pltpu.SMEM)


def hbm():
    return pl.BlockSpec(memory_space=pltpu.HBM)


def in_hbm(array):
    return pltpu.with_memory_space_constraint(array, pltpu.HBM)


def params(mib):
    return pltpu.CompilerParams(vmem_limit_bytes=mib << 20)


def face_weights(courant):
    speed = jnp.abs(courant)
    rest = 1.0 - speed
    mid = courant * rest * rest
    far = -courant * speed * rest
    centre = courant * speed * (3.0 - 2.0 * speed)
    positive = courant > 0.0
    far_low = jnp.where(positive, far, 0.0)
    far_high = far - far_low
    centre_low = jnp.where(positive, centre, 0.0)
    centre_high = centre - centre_low
    small, large = 1.0 / 12.0, 7.0 / 12.0
    return [
        -small * far_low,
        large * far_low - small * mid,
        large * (mid + far_low) - small * far_high + centre_low,
        large * (mid + far_high) - small * far_low + centre_high,
        large * far_high - small * mid,
        -small * far_high,
    ]


def cell_weights(before, after):
    zero = jnp.zeros_like(before[0])
    return [a - b for a, b in zip(before + [zero], [zero] + after)]


def block_transpose(rows, lane):
    low = lane < 64
    even = (lane & 32) == 0
    r0, r1, r2, r3 = rows
    b0 = jnp.where(low, r0, pltpu.roll(r2, 64, 1))
    b2 = jnp.where(low, pltpu.roll(r0, 64, 1), r2)
    b1 = jnp.where(low, r1, pltpu.roll(r3, 64, 1))
    b3 = jnp.where(low, pltpu.roll(r1, 64, 1), r3)
    return (
        jnp.where(even, b0, pltpu.roll(b1, 32, 1)),
        jnp.where(even, pltpu.roll(b0, 96, 1), b1),
        jnp.where(even, b2, pltpu.roll(b3, 32, 1)),
        jnp.where(even, pltpu.roll(b2, 96, 1), b3),
    )


def split3(values):
    high = values.astype(BF16).astype(F32)
    rest = values - high
    mid = rest.astype(BF16).astype(F32)
    return high, mid, rest - mid


def pack_kernel(levels, width, quarter, pieces, *refs):
    even = (refs[0][0, 0] & 1) == 0
    refs = refs[1:]
    count = (len(refs) - 3) // 2
    sources, (a_ref, b_ref), targets = refs[:count], refs[count : count + 2], refs[count + 2 : -1]
    sems = refs[-1]
    x_ref, u_ref = targets[0], targets[1]
    grid = levels * width
    part = quarter // pieces
    small, large = [], []
    for i in range(1, count):
        small.append(pltpu.make_async_copy(sources[i], targets[i], sems.at[pieces + i - 1]))
    for i in range(pieces):
        rows = pl.ds(i * part * grid, part * grid)
        large.append(pltpu.make_async_copy(sources[0].at[rows], x_ref.at[rows], sems.at[i]))
    small[0].start()
    for copy in large + small[1:]:
        copy.start()
    small[0].wait()
    row = levels * 3 * quarter
    parts = split3(u_ref[pl.ds(0, levels, stride=width), :])
    parts = jnp.concatenate(parts + (jnp.zeros_like(parts[0]),), axis=0)
    a_ref[row : row + 4 * levels, :] = parts.astype(BF16)
    b_ref[row : row + 4 * levels, :] = parts.astype(BF16)
    for i in range(pieces):
        large[i].wait()
        for level in range(levels):
            start = i * part * grid + level * width
            cells = [x_ref[pl.ds(start + c, part, stride=grid), :] for c in range(width)]
            for c in range(3):
                row = (level * 3 + c) * quarter + i * part
                low, high = cells[c], cells[width - 3 + c]
                a_ref[row : row + part, :] = jnp.where(even, high, low).astype(BF16)
                b_ref[row : row + part, :] = jnp.where(even, low, high).astype(BF16)
    for copy in small[1:]:
        copy.wait()


def local_kernel(
    levels,
    width,
    quarter,
    flag_ref,
    x_ref,
    cycle_ref,
    edge_ref,
    entry_ref,
    sun_ref,
    mix_ref,
    base_ref,
    weight_ref,
    table_ref,
    turn_ref,
    own_ref,
    tab_ref,
):
    grid = levels * width
    chunk = 32
    row = lax.broadcasted_iota(jnp.int32, (LANES, LANES), 0)
    col = lax.broadcasted_iota(jnp.int32, (LANES, LANES), 1)
    for side in range(2):
        flag = jnp.broadcast_to(flag_ref[0:1, side : side + 1], (LANES, LANES))
        source = jnp.where(flag > 0, LANES - 1 - col, col)
        turn_ref[side] = jnp.where(row == source, 1.0, 0.0).astype(BF16)
    entries = entry_ref.shape[0]
    tab_ref[...] = jnp.zeros_like(tab_ref)
    tab_ref[0:entries, :] = entry_ref[...].astype(F32)
    tab_ref[entries : entries + 1, :] = sun_ref[...].astype(F32)
    for i, part in enumerate(split3(mix_ref[...])):
        row = entries + 1 + i * (levels - 1)
        tab_ref[row : row + levels - 1, :] = part
    table_ref[...] = tab_ref[...].astype(BF16)
    shape = (grid, LANES)
    lane = lax.broadcasted_iota(jnp.int32, shape, 1)
    column = lax.broadcasted_iota(jnp.int32, shape, 0) % width
    faces = face_weights(cycle_ref[...])
    after = [jnp.where(column == width - 1, 0.0, pltpu.roll(w, grid - 1, 0)) for w in faces]
    across = cell_weights(faces, after)
    for k in range(7):
        weight_ref[k] = across[k]
    faces = face_weights(jnp.where(lane == 0, 0.0, edge_ref[...]))
    along = cell_weights(faces, [pltpu.roll(w, LANES - 1, 1) for w in faces])
    low3, low2, low1, here, high1, high2, high3 = along
    here = jnp.where(lane == 0, here + low1 + low2 + low3, here)
    low1 = jnp.where(lane == 1, low1 + low2 + low3, low1)
    low2 = jnp.where(lane == 2, low2 + low3, low2)
    here = jnp.where(lane == LANES - 1, here + high1 + high2 + high3, here)
    high1 = jnp.where(lane == LANES - 2, high1 + high2 + high3, high1)
    high2 = jnp.where(lane == LANES - 3, high2 + high3, high2)
    own_ref[0] = jnp.where(lane < 3, 0.0, low3)
    own_ref[1] = jnp.where(lane < 2, 0.0, low2)
    own_ref[2] = jnp.where(lane < 1, 0.0, low1)
    own_ref[3] = 1.0 + here + across[3]
    own_ref[4] = jnp.where(lane > LANES - 2, 0.0, high1)
    own_ref[5] = jnp.where(lane > LANES - 3, 0.0, high2)
    own_ref[6] = jnp.where(lane > LANES - 4, 0.0, high3)
    for level in range(levels):
        for start in range(0, quarter, chunk):
            cells = [
                x_ref[pl.ds(start * grid + level * width + col, chunk, stride=grid), :]
                for col in range(width)
            ]
            for col in range(width):
                cell = level * width + col
                total = cells[col] * own_ref[3, cell : cell + 1, :]
                for k in (-3, -2, -1, 1, 2, 3):
                    moved = pltpu.roll(cells[col], (-k) % LANES, 1)
                    total = total + moved * own_ref[3 + k, cell : cell + 1, :]
                    if 0 <= col + k < width:
                        total = total + cells[col + k] * weight_ref[3 + k, cell : cell + 1, :]
                base_ref[cell, start : start + chunk, :] = total


def maps_kernel(rank_ref, map_ref, off_ref, full_ref, last_ref, shift_ref, scratch_ref):
    rank = rank_ref[0, 0]
    count, quarter, species = full_ref.shape
    parts = species // quarter
    entries = count // parts
    row = lax.broadcasted_iota(jnp.int32, (species, species), 0)
    col = lax.broadcasted_iota(jnp.int32, (species, species), 1)
    shuffle = jnp.where(row == (col ^ (rank * quarter)), 1.0, 0.0).astype(BF16)
    for e in range(entries):
        moved = jnp.dot(map_ref[e], shuffle, preferred_element_type=F32).astype(BF16)
        for k in range(parts):
            scratch_ref[e * parts + k] = moved[k * quarter : (k + 1) * quarter, :]
    for e in range(entries):
        for k in range(parts):
            block = scratch_ref[e * parts + (rank ^ k)]
            full_ref[e * parts + k] = block
            if k < 2:
                last_ref[2 * e + k] = block
    for k in range(parts):
        shift_ref[k] = off_ref[rank ^ k]


def halo_terms(levels, width, quarter, side, level, start, chunk, closing, x_ref, weight_ref, turn_ref, halo_of):
    grid = levels * width
    begins = [(level * 3 + i) * quarter + start for i in range(3)]
    values = jnp.concatenate([halo_of(begin, chunk) for begin in begins], axis=0)
    values = jnp.dot(values, turn_ref[side], preferred_element_type=F32)
    offset = width if side else -3
    outer = {offset + i: values[i * chunk : (i + 1) * chunk] for i in range(3)}
    terms = []
    for c in range(width):
        cell = level * width + c
        total = None
        for k in range(-3, 4):
            if c + k in outer and not (c == width - 1 and k == 3):
                term = outer[c + k] * weight_ref[3 + k, cell : cell + 1, :]
                total = term if total is None else total + term
        if side and c == width - 1:
            for k in range(-3, 3):
                if width + k in outer:
                    value = outer[width + k]
                else:
                    begin = start * grid + level * width + width + k
                    value = x_ref[pl.ds(begin, chunk, stride=grid), :]
                total = total - value * closing[3 + k][level : level + 1, :]
        terms.append(total)
    return terms


def closing_weights(levels, quarter, turn_ref, halo_of):
    split = halo_of(levels * 3 * quarter, 4 * levels)
    split = jnp.dot(split, turn_ref[1], preferred_element_type=F32)
    return face_weights(split[0:levels] + split[levels : 2 * levels] + split[2 * levels : 3 * levels])


def near_kernel(
    levels, width, quarter, tile_ref, x_ref, base_ref, weight_ref, turn_ref, a0_ref, a1_ref, near_ref
):
    chunk = 32
    even = (tile_ref[0, 0] & 1) == 0

    def halo_of(begin, size):
        return a0_ref[begin : begin + size, :] + a1_ref[begin : begin + size, :]

    def work(side):
        closing = closing_weights(levels, quarter, turn_ref, halo_of) if side else None
        for level in range(levels):
            for start in range(0, quarter, chunk):
                terms = halo_terms(
                    levels, width, quarter, side, level, start, chunk, closing,
                    x_ref, weight_ref, turn_ref, halo_of,
                )
                for c in range(width):
                    cell = level * width + c
                    total = base_ref[cell, start : start + chunk, :]
                    if terms[c] is not None:
                        total = total + terms[c]
                    near_ref[cell, start : start + chunk, :] = total

    pl.when(even)(lambda: work(1))
    pl.when(jnp.logical_not(even))(lambda: work(0))


def flow_kernel(
    levels,
    width,
    quarter,
    rank_ref,
    tile_ref,
    x_ref,
    near_ref,
    weight_ref,
    table_ref,
    turn_ref,
    b_ref,
    mine_ref,
    other_ref,
):
    chunk = 32
    half = width // 2
    first_core = (rank_ref[0, 0] & 1) == 0
    even = (tile_ref[0, 0] & 1) == 0

    def halo_of(begin, size):
        return b_ref[begin : begin + size, :]

    def work(side):
        closing = closing_weights(levels, quarter, turn_ref, halo_of) if side else None
        for level in range(levels):
            for start in range(0, quarter, chunk):
                terms = halo_terms(
                    levels, width, quarter, side, level, start, chunk, closing,
                    x_ref, weight_ref, turn_ref, halo_of,
                )
                moved = []
                for c in range(width):
                    total = near_ref[level * width + c, start : start + chunk, :]
                    moved.append(total if terms[c] is None else total + terms[c])
                for k in range(half):
                    low, high = moved[k], moved[half + k]
                    begin = (level * half + k) * quarter + start
                    mine_ref[begin : begin + chunk, :] = jnp.where(first_core, low, high).astype(BF16)
                    other_ref[begin : begin + chunk, :] = jnp.where(first_core, high, low).astype(BF16)

    pl.when(even)(lambda: work(0))
    pl.when(jnp.logical_not(even))(lambda: work(1))
    begin = levels * half * quarter
    mine_ref[begin : begin + TABLE_ROWS, :] = table_ref[...]
    other_ref[begin : begin + TABLE_ROWS, :] = table_ref[...]


def tables_of(rank, tails):
    lane = lax.broadcasted_iota(jnp.int32, (TABLE_ROWS, LANES), 1)
    t0, t1, t2, t3 = [t.astype(F32) for t in tails]
    odd = (rank & 1) > 0
    t0, t1 = jnp.where(odd, t1, t0), jnp.where(odd, t0, t1)
    t2, t3 = jnp.where(odd, t3, t2), jnp.where(odd, t2, t3)
    upper = (rank & 2) > 0
    t0, t2 = jnp.where(upper, t2, t0), jnp.where(upper, t0, t2)
    t1, t3 = jnp.where(upper, t3, t1), jnp.where(upper, t1, t3)
    return block_transpose((t0, t1, t2, t3), lane)


def chem_kernel(
    levels,
    width,
    quarter,
    entries,
    substeps,
    rank_ref,
    block0_ref,
    block1_ref,
    block2_ref,
    block3_ref,
    tail0_ref,
    tail1_ref,
    tail2_ref,
    tail3_ref,
    away_ref,
    map_ref,
    last_ref,
    off_ref,
    keep_ref,
    give_ref,
    spare_ref,
    flag_ref,
    chem_ref,
):
    block_refs = (block0_ref, block1_ref, block2_ref, block3_ref)
    tail_refs = (tail0_ref, tail1_ref, tail2_ref, tail3_ref)
    parts = len(block_refs)
    species = parts * quarter
    half = width // 2
    even = (rank_ref[0, 0] & 1) == 0
    tables = tables_of(rank_ref[0, 0], [r[...] for r in tail_refs])
    columns = [jnp.where(even, tables[k], tables[half + k]) for k in range(half)]

    def row_of(index):
        return jnp.concatenate([columns[k][index : index + 1, :] for k in range(half)], axis=1)

    def block(part, group):
        return block_refs[part][group * quarter : (group + 1) * quarter, :]

    sun = substeps * levels
    lit = row_of(sun) > 0.0
    suns = jnp.concatenate([t[sun : sun + 1, :] for t in tables], axis=0)
    any_lit = jnp.max(suns) > 0.0
    flag_ref[...] = jnp.broadcast_to(jnp.max(suns, axis=(0, 1), keepdims=True), flag_ref.shape).astype(jnp.int32)
    away = [jnp.where(even, tables[half + k], tables[k]) for k in range(half)]

    @pl.when(any_lit)
    def lit_tile():
        start = []
        for level in range(levels):
            cells = [
                jnp.concatenate([block(p, level * half + k) for p in range(parts)], axis=0)
                for k in range(half)
            ]
            start.append(jnp.concatenate(cells, axis=1))
        state = list(start)
        for step in range(substeps):
            final = step == substeps - 1
            rows = 2 * quarter if final else species
            matrix = last_ref[...] if final else map_ref[...]
            for level in range(levels):
                product = jnp.dot(matrix, state[level], preferred_element_type=F32)
                entry = row_of(step * levels + level)
                chosen = product[0:rows] + off_ref[0:rows, 0:1]
                for e in range(1, entries):
                    chosen = jnp.where(
                        entry == float(e),
                        product[e * rows : (e + 1) * rows] + off_ref[0:rows, e : e + 1],
                        chosen,
                    )
                chosen = jnp.maximum(chosen, 0.0)
                if not final:
                    state[level] = chosen.astype(BF16)
                    continue
                chem = jnp.where(lit, chosen, start[level][0:rows].astype(F32))
                for k in range(half):
                    chem_ref[level * half + k] = chem[:, k * LANES : (k + 1) * LANES]

    def solve(columns, source_of, out_ref):
        chunk = 32
        for k in range(half):
            pieces = [
                columns[k][sun + 1 + i * (levels - 1) : sun + 1 + (i + 1) * (levels - 1), :]
                for i in range(3)
            ]
            mixed = pieces[0] + pieces[1] + pieces[2]
            mixing = [mixed[i : i + 1, :] for i in range(levels - 1)]
            inverse, ratio = [], []
            for level in range(levels):
                diagonal = 1.0
                if level > 0:
                    diagonal = diagonal + mixing[level - 1]
                if level < levels - 1:
                    diagonal = diagonal + mixing[level]
                if level > 0:
                    diagonal = diagonal - mixing[level - 1] * ratio[level - 1]
                inverse.append(1.0 / diagonal)
                if level < levels - 1:
                    ratio.append(mixing[level] * inverse[level])
            for begin in range(0, quarter, chunk):
                solved = []
                for level in range(levels):
                    value = source_of(level * half + k, begin, chunk)
                    if level > 0:
                        value = value + mixing[level - 1] * solved[-1]
                    solved.append(value * inverse[level])
                for level in range(levels - 2, -1, -1):
                    solved[level] = solved[level] + ratio[level] * solved[level + 1]
                for level in range(levels):
                    place = begin * levels * half + level * half + k
                    out_ref[pl.ds(place, chunk, stride=levels * half), :] = solved[level]

    @pl.when(any_lit)
    def lit_mixing():
        for p, out_ref in enumerate((keep_ref, give_ref)):
            solve(
                columns,
                lambda g, begin, chunk: chem_ref[
                    g, p * quarter + begin : p * quarter + begin + chunk, :
                ],
                out_ref,
            )

    @pl.when(jnp.logical_not(any_lit))
    def dark_mixing():
        for tabs, ref, out_ref in (
            (columns, block0_ref, keep_ref),
            (away, away_ref, spare_ref),
        ):
            solve(
                tabs,
                lambda g, begin, chunk: ref[
                    g * quarter + begin : g * quarter + begin + chunk, :
                ].astype(F32),
                out_ref,
            )


def keep_kernel(rank_ref, keep_ref, out_hbm, sem):
    copy = pltpu.make_async_copy(keep_ref, out_hbm.at[:, rank_ref[0, 0] & 1], sem)
    copy.start()
    copy.wait()


def fill_kernel(rank_ref, got_ref, part_hbm, out_hbm, sem):
    del part_hbm
    copy = pltpu.make_async_copy(got_ref, out_hbm.at[:, 1 - (rank_ref[0, 0] & 1)], sem)
    copy.start()
    copy.wait()


def both_kernel(rank_ref, keep_ref, spare_ref, out_hbm, sems):
    core = rank_ref[0, 0] & 1
    copies = [
        pltpu.make_async_copy(keep_ref, out_hbm.at[:, core], sems.at[0]),
        pltpu.make_async_copy(spare_ref, out_hbm.at[:, 1 - core], sems.at[1]),
    ]
    for copy in copies:
        copy.start()
    for copy in copies:
        copy.wait()


def shards(
    tracers,
    courant_cycle,
    courant_edge,
    seam_flags,
    sunlit,
    table_entry,
    linear_maps,
    offsets,
    mixing,
):
    quarter, levels, width, length = tracers.shape
    grid = levels * width
    substeps = table_entry.shape[0]
    entries, species, _ = linear_maps.shape
    count = lax.axis_size("tile")
    parts = lax.axis_size("trc")
    pairs = [(i, i ^ 1) for i in range(count)]
    seams = [(i, (i + (1 if i % 2 else -1)) % count) for i in range(count)]
    tile = lax.axis_index("tile").astype(jnp.int32).reshape(1, 1)
    halo = levels * 3 * quarter
    pieces = 4
    shape = jax.ShapeDtypeStruct
    brought = [
        tracers.reshape(quarter * grid, length),
        courant_cycle.reshape(grid, length),
        courant_edge.reshape(grid, length),
        table_entry,
        sunlit,
        mixing,
        seam_flags,
    ]
    to_a, to_b, x, cycle, edge, entry, sun, mix, flags = pl.pallas_call(
        functools.partial(pack_kernel, levels, width, quarter, pieces),
        out_shape=(
            shape((halo + 4 * levels, length), BF16),
            shape((halo + 4 * levels, length), BF16),
            *[shape(array.shape, array.dtype) for array in brought],
        ),
        in_specs=[smem()] + [hbm()] * len(brought),
        out_specs=(vmem(),) * (2 + len(brought)),
        scratch_shapes=[pltpu.SemaphoreType.DMA((pieces + len(brought) - 1,))],
        compiler_params=params(8),
        name="pack",
    )(tile, *[in_hbm(array) for array in brought])
    from_a0 = lax.ppermute(to_a, "tile", pairs[:2])
    from_b = lax.ppermute(to_b, "tile", seams)
    from_a1 = lax.ppermute(to_a, "tile", pairs[2:])
    rank = lax.axis_index("trc").astype(jnp.int32).reshape(1, 1)
    base, weights, table, turns = pl.pallas_call(
        functools.partial(local_kernel, levels, width, quarter),
        out_shape=(
            shape((grid, quarter, length), F32),
            shape((7, grid, length), F32),
            shape((TABLE_ROWS, length), BF16),
            shape((2, length, length), BF16),
        ),
        in_specs=[vmem()] * 7,
        out_specs=(vmem(),) * 4,
        scratch_shapes=[
            pltpu.VMEM((7, grid, length), F32),
            pltpu.VMEM((TABLE_ROWS, length), F32),
        ],
        compiler_params=params(8),
        cost_estimate=pl.CostEstimate(flops=4000000, bytes_accessed=1 << 20, transcendentals=0),
        name="local",
    )(
        flags,
        x,
        cycle,
        edge,
        entry.reshape(substeps * levels, length),
        sun.reshape(1, length),
        mix.reshape(levels - 1, length),
    )
    rows = grid // 2 * quarter
    near = pl.pallas_call(
        functools.partial(near_kernel, levels, width, quarter),
        out_shape=shape((grid, quarter, length), F32),
        in_specs=[smem()] + [vmem()] * 6,
        out_specs=vmem(),
        compiler_params=params(8),
        name="near",
    )(tile, x, base, weights, turns, from_a0, from_a1)
    mine, other = pl.pallas_call(
        functools.partial(flow_kernel, levels, width, quarter),
        out_shape=(shape((rows + TABLE_ROWS, length), BF16),) * 2,
        in_specs=[smem()] * 2 + [vmem()] * 6,
        out_specs=(vmem(),) * 2,
        compiler_params=params(8),
        name="flow",
    )(rank, tile, x, near, weights, table, turns, from_b)
    swap = {k: [(i, i ^ k) for i in range(parts)] for k in (1, 2, 3)}
    second = lax.ppermute(mine, "trc", swap[2])
    third = lax.ppermute(other, "trc", swap[3])
    first = lax.ppermute(other, "trc", swap[1])
    full, last, shift = pl.pallas_call(
        maps_kernel,
        out_shape=(
            shape((entries * parts, quarter, species), BF16),
            shape((2 * entries, quarter, species), BF16),
            shape((parts, quarter, entries), F32),
        ),
        in_specs=[smem()] + [vmem()] * 2,
        out_specs=(vmem(),) * 3,
        scratch_shapes=[pltpu.VMEM((entries * parts, quarter, species), BF16)],
        compiler_params=params(8),
        cost_estimate=pl.CostEstimate(flops=4000000, bytes_accessed=1 << 20, transcendentals=0),
        name="maps",
    )(rank, linear_maps, offsets.T.reshape(parts, quarter, entries))
    blocks = [mine, first, second, third]
    keep, give, spare, flag = pl.pallas_call(
        functools.partial(chem_kernel, levels, width, quarter, entries, substeps),
        out_shape=(shape((rows, length), F32),) * 3 + (shape((8, length), jnp.int32),),
        in_specs=[smem()] + [vmem()] * 12,
        out_specs=(vmem(),) * 4,
        scratch_shapes=[pltpu.VMEM((grid // 2, 2 * quarter, length), F32)],
        compiler_params=params(24),
        name="chem",
    )(
        rank,
        *blocks,
        *[b[rows:] for b in blocks],
        other,
        full.reshape(entries * species, species),
        last.reshape(2 * entries * quarter, species),
        shift.reshape(species, entries),
    )
    pair = (quarter * levels, width // 2, length)
    whole = shape((quarter * levels, 2, width // 2, length), F32)

    def lit_end(rank, keep, give, spare):
        got = lax.ppermute(give, "trc", swap[1])
        part = pl.pallas_call(
            keep_kernel,
            out_shape=whole,
            in_specs=[smem(), vmem()],
            out_specs=hbm(),
            scratch_shapes=[pltpu.SemaphoreType.DMA],
            compiler_params=params(4),
            cost_estimate=pl.CostEstimate(flops=1000000, bytes_accessed=1 << 19, transcendentals=0),
            name="keep",
        )(rank, keep.reshape(pair))
        return pl.pallas_call(
            fill_kernel,
            out_shape=whole,
            in_specs=[smem(), vmem(), hbm()],
            out_specs=hbm(),
            scratch_shapes=[pltpu.SemaphoreType.DMA],
            input_output_aliases={2: 0},
            compiler_params=params(4),
            name="fill",
        )(rank, got.reshape(pair), part)

    def dark_end(rank, keep, give, spare):
        return pl.pallas_call(
            both_kernel,
            out_shape=whole,
            in_specs=[smem(), vmem(), vmem()],
            out_specs=hbm(),
            scratch_shapes=[pltpu.SemaphoreType.DMA((2,))],
            compiler_params=params(4),
            name="both",
        )(rank, keep.reshape(pair), spare.reshape(pair))

    out = lax.switch(flag[0, 0], (dark_end, lit_end), rank, keep, give, spare)
    return out.reshape(quarter, levels, width, length)


def solution(mesh):
    placed = (
        P("trc", None, "tile", None),
        P(None, "tile", None),
        P(None, "tile", None),
        P("tile", None),
        P("tile", "trc"),
        P(None, None, "tile", "trc"),
        P(),
        P(),
        P(None, "tile", "trc"),
    )
    return jax.shard_map(
        shards, mesh=mesh, in_specs=placed, out_specs=P("trc", None, "tile", None), check_vma=False
    )
```

```python
import functools

import jax
import jax.numpy as jnp
from jax import lax
from jax.experimental import pallas as pl
from jax.experimental.pallas import tpu as pltpu
from jax.sharding import PartitionSpec as P

F32 = jnp.float32
BF16 = jnp.bfloat16
LANES = 128
TABLE_ROWS = 32


def vmem():
    return pl.BlockSpec(memory_space=pltpu.VMEM)


def smem():
    return pl.BlockSpec(memory_space=pltpu.SMEM)


def hbm():
    return pl.BlockSpec(memory_space=pltpu.HBM)


def in_hbm(array):
    return pltpu.with_memory_space_constraint(array, pltpu.HBM)


def params(mib):
    return pltpu.CompilerParams(vmem_limit_bytes=mib << 20)


def face_weights(courant):
    speed = jnp.abs(courant)
    rest = 1.0 - speed
    mid = courant * rest * rest
    far = -courant * speed * rest
    centre = courant * speed * (3.0 - 2.0 * speed)
    positive = courant > 0.0
    far_low = jnp.where(positive, far, 0.0)
    far_high = far - far_low
    centre_low = jnp.where(positive, centre, 0.0)
    centre_high = centre - centre_low
    small, large = 1.0 / 12.0, 7.0 / 12.0
    return [
        -small * far_low,
        large * far_low - small * mid,
        large * (mid + far_low) - small * far_high + centre_low,
        large * (mid + far_high) - small * far_low + centre_high,
        large * far_high - small * mid,
        -small * far_high,
    ]


def cell_weights(before, after):
    zero = jnp.zeros_like(before[0])
    return [a - b for a, b in zip(before + [zero], [zero] + after)]


def block_transpose(rows, lane):
    low = lane < 64
    even = (lane & 32) == 0
    r0, r1, r2, r3 = rows
    b0 = jnp.where(low, r0, pltpu.roll(r2, 64, 1))
    b2 = jnp.where(low, pltpu.roll(r0, 64, 1), r2)
    b1 = jnp.where(low, r1, pltpu.roll(r3, 64, 1))
    b3 = jnp.where(low, pltpu.roll(r1, 64, 1), r3)
    return (
        jnp.where(even, b0, pltpu.roll(b1, 32, 1)),
        jnp.where(even, pltpu.roll(b0, 96, 1), b1),
        jnp.where(even, b2, pltpu.roll(b3, 32, 1)),
        jnp.where(even, pltpu.roll(b2, 96, 1), b3),
    )


def split3(values):
    high = values.astype(BF16).astype(F32)
    rest = values - high
    mid = rest.astype(BF16).astype(F32)
    return high, mid, rest - mid


def pack_kernel(levels, width, quarter, pieces, *refs):
    even = (refs[0][0, 0] & 1) == 0
    refs = refs[1:]
    count = (len(refs) - 3) // 2
    sources, (a_ref, b_ref), targets = refs[:count], refs[count : count + 2], refs[count + 2 : -1]
    sems = refs[-1]
    x_ref, u_ref = targets[0], targets[1]
    grid = levels * width
    part = quarter // pieces
    small, large = [], []
    for i in range(1, count):
        small.append(pltpu.make_async_copy(sources[i], targets[i], sems.at[pieces + i - 1]))
    for i in range(pieces):
        rows = pl.ds(i * part * grid, part * grid)
        large.append(pltpu.make_async_copy(sources[0].at[rows], x_ref.at[rows], sems.at[i]))
    small[0].start()
    for copy in large + small[1:]:
        copy.start()
    small[0].wait()
    row = levels * 3 * quarter
    parts = split3(u_ref[pl.ds(0, levels, stride=width), :])
    parts = jnp.concatenate(parts + (jnp.zeros_like(parts[0]),), axis=0)
    a_ref[row : row + 4 * levels, :] = parts.astype(BF16)
    b_ref[row : row + 4 * levels, :] = parts.astype(BF16)
    for i in range(pieces):
        large[i].wait()
        for level in range(levels):
            start = i * part * grid + level * width
            cells = [x_ref[pl.ds(start + c, part, stride=grid), :] for c in range(width)]
            for c in range(3):
                row = (level * 3 + c) * quarter + i * part
                low, high = cells[c], cells[width - 3 + c]
                a_ref[row : row + part, :] = jnp.where(even, high, low).astype(BF16)
                b_ref[row : row + part, :] = jnp.where(even, low, high).astype(BF16)
    for copy in small[1:]:
        copy.wait()


def local_kernel(
    levels,
    width,
    quarter,
    flag_ref,
    x_ref,
    cycle_ref,
    edge_ref,
    entry_ref,
    sun_ref,
    mix_ref,
    base_ref,
    weight_ref,
    table_ref,
    turn_ref,
    own_ref,
    tab_ref,
):
    grid = levels * width
    chunk = 32
    row = lax.broadcasted_iota(jnp.int32, (LANES, LANES), 0)
    col = lax.broadcasted_iota(jnp.int32, (LANES, LANES), 1)
    for side in range(2):
        flag = jnp.broadcast_to(flag_ref[0:1, side : side + 1], (LANES, LANES))
        source = jnp.where(flag > 0, LANES - 1 - col, col)
        turn_ref[side] = jnp.where(row == source, 1.0, 0.0).astype(BF16)
    entries = entry_ref.shape[0]
    tab_ref[...] = jnp.zeros_like(tab_ref)
    tab_ref[0:entries, :] = entry_ref[...].astype(F32)
    tab_ref[entries : entries + 1, :] = sun_ref[...].astype(F32)
    for i, part in enumerate(split3(mix_ref[...])):
        row = entries + 1 + i * (levels - 1)
        tab_ref[row : row + levels - 1, :] = part
    table_ref[...] = tab_ref[...].astype(BF16)
    shape = (grid, LANES)
    lane = lax.broadcasted_iota(jnp.int32, shape, 1)
    column = lax.broadcasted_iota(jnp.int32, shape, 0) % width
    faces = face_weights(cycle_ref[...])
    after = [jnp.where(column == width - 1, 0.0, pltpu.roll(w, grid - 1, 0)) for w in faces]
    across = cell_weights(faces, after)
    for k in range(7):
        weight_ref[k] = across[k]
    faces = face_weights(jnp.where(lane == 0, 0.0, edge_ref[...]))
    along = cell_weights(faces, [pltpu.roll(w, LANES - 1, 1) for w in faces])
    low3, low2, low1, here, high1, high2, high3 = along
    here = jnp.where(lane == 0, here + low1 + low2 + low3, here)
    low1 = jnp.where(lane == 1, low1 + low2 + low3, low1)
    low2 = jnp.where(lane == 2, low2 + low3, low2)
    here = jnp.where(lane == LANES - 1, here + high1 + high2 + high3, here)
    high1 = jnp.where(lane == LANES - 2, high1 + high2 + high3, high1)
    high2 = jnp.where(lane == LANES - 3, high2 + high3, high2)
    own_ref[0] = jnp.where(lane < 3, 0.0, low3)
    own_ref[1] = jnp.where(lane < 2, 0.0, low2)
    own_ref[2] = jnp.where(lane < 1, 0.0, low1)
    own_ref[3] = 1.0 + here + across[3]
    own_ref[4] = jnp.where(lane > LANES - 2, 0.0, high1)
    own_ref[5] = jnp.where(lane > LANES - 3, 0.0, high2)
    own_ref[6] = jnp.where(lane > LANES - 4, 0.0, high3)
    for level in range(levels):
        for start in range(0, quarter, chunk):
            cells = [
                x_ref[pl.ds(start * grid + level * width + col, chunk, stride=grid), :]
                for col in range(width)
            ]
            for col in range(width):
                cell = level * width + col
                total = cells[col] * own_ref[3, cell : cell + 1, :]
                for k in (-3, -2, -1, 1, 2, 3):
                    moved = pltpu.roll(cells[col], (-k) % LANES, 1)
                    total = total + moved * own_ref[3 + k, cell : cell + 1, :]
                    if 0 <= col + k < width:
                        total = total + cells[col + k] * weight_ref[3 + k, cell : cell + 1, :]
                base_ref[cell, start : start + chunk, :] = total


def maps_kernel(rank_ref, map_ref, off_ref, full_ref, last_ref, shift_ref, scratch_ref):
    rank = rank_ref[0, 0]
    count, quarter, species = full_ref.shape
    parts = species // quarter
    entries = count // parts
    row = lax.broadcasted_iota(jnp.int32, (species, species), 0)
    col = lax.broadcasted_iota(jnp.int32, (species, species), 1)
    shuffle = jnp.where(row == (col ^ (rank * quarter)), 1.0, 0.0).astype(BF16)
    for e in range(entries):
        moved = jnp.dot(map_ref[e], shuffle, preferred_element_type=F32).astype(BF16)
        for k in range(parts):
            scratch_ref[e * parts + k] = moved[k * quarter : (k + 1) * quarter, :]
    for e in range(entries):
        for k in range(parts):
            block = scratch_ref[e * parts + (rank ^ k)]
            full_ref[e * parts + k] = block
            if k < 2:
                last_ref[2 * e + k] = block
    for k in range(parts):
        shift_ref[k] = off_ref[rank ^ k]


def halo_terms(levels, width, quarter, side, level, start, chunk, closing, x_ref, weight_ref, turn_ref, halo_of):
    grid = levels * width
    begins = [(level * 3 + i) * quarter + start for i in range(3)]
    values = jnp.concatenate([halo_of(begin, chunk) for begin in begins], axis=0)
    values = jnp.dot(values, turn_ref[side], preferred_element_type=F32)
    offset = width if side else -3
    outer = {offset + i: values[i * chunk : (i + 1) * chunk] for i in range(3)}
    terms = []
    for c in range(width):
        cell = level * width + c
        total = None
        for k in range(-3, 4):
            if c + k in outer and not (c == width - 1 and k == 3):
                term = outer[c + k] * weight_ref[3 + k, cell : cell + 1, :]
                total = term if total is None else total + term
        if side and c == width - 1:
            for k in range(-3, 3):
                if width + k in outer:
                    value = outer[width + k]
                else:
                    begin = start * grid + level * width + width + k
                    value = x_ref[pl.ds(begin, chunk, stride=grid), :]
                total = total - value * closing[3 + k][level : level + 1, :]
        terms.append(total)
    return terms


def closing_weights(levels, quarter, turn_ref, halo_of):
    split = halo_of(levels * 3 * quarter, 4 * levels)
    split = jnp.dot(split, turn_ref[1], preferred_element_type=F32)
    return face_weights(split[0:levels] + split[levels : 2 * levels] + split[2 * levels : 3 * levels])


def near_kernel(
    levels, width, quarter, tile_ref, x_ref, base_ref, weight_ref, turn_ref, a0_ref, a1_ref, near_ref
):
    chunk = 32
    even = (tile_ref[0, 0] & 1) == 0

    def halo_of(begin, size):
        return a0_ref[begin : begin + size, :] + a1_ref[begin : begin + size, :]

    def work(side):
        closing = closing_weights(levels, quarter, turn_ref, halo_of) if side else None
        for level in range(levels):
            for start in range(0, quarter, chunk):
                terms = halo_terms(
                    levels, width, quarter, side, level, start, chunk, closing,
                    x_ref, weight_ref, turn_ref, halo_of,
                )
                for c in range(width):
                    cell = level * width + c
                    total = base_ref[cell, start : start + chunk, :]
                    if terms[c] is not None:
                        total = total + terms[c]
                    near_ref[cell, start : start + chunk, :] = total

    pl.when(even)(lambda: work(1))
    pl.when(jnp.logical_not(even))(lambda: work(0))


def flow_kernel(
    levels,
    width,
    quarter,
    rank_ref,
    tile_ref,
    x_ref,
    near_ref,
    weight_ref,
    table_ref,
    turn_ref,
    b_ref,
    mine_ref,
    other_ref,
):
    chunk = 32
    half = width // 2
    first_core = (rank_ref[0, 0] & 1) == 0
    even = (tile_ref[0, 0] & 1) == 0

    def halo_of(begin, size):
        return b_ref[begin : begin + size, :]

    def work(side):
        closing = closing_weights(levels, quarter, turn_ref, halo_of) if side else None
        for level in range(levels):
            for start in range(0, quarter, chunk):
                terms = halo_terms(
                    levels, width, quarter, side, level, start, chunk, closing,
                    x_ref, weight_ref, turn_ref, halo_of,
                )
                moved = []
                for c in range(width):
                    total = near_ref[level * width + c, start : start + chunk, :]
                    moved.append(total if terms[c] is None else total + terms[c])
                for k in range(half):
                    low, high = moved[k], moved[half + k]
                    begin = (level * half + k) * quarter + start
                    mine_ref[begin : begin + chunk, :] = jnp.where(first_core, low, high).astype(BF16)
                    other_ref[begin : begin + chunk, :] = jnp.where(first_core, high, low).astype(BF16)

    pl.when(even)(lambda: work(0))
    pl.when(jnp.logical_not(even))(lambda: work(1))
    begin = levels * half * quarter
    mine_ref[begin : begin + TABLE_ROWS, :] = table_ref[...]
    other_ref[begin : begin + TABLE_ROWS, :] = table_ref[...]


def tables_of(rank, tails):
    lane = lax.broadcasted_iota(jnp.int32, (TABLE_ROWS, LANES), 1)
    t0, t1, t2, t3 = [t.astype(F32) for t in tails]
    odd = (rank & 1) > 0
    t0, t1 = jnp.where(odd, t1, t0), jnp.where(odd, t0, t1)
    t2, t3 = jnp.where(odd, t3, t2), jnp.where(odd, t2, t3)
    upper = (rank & 2) > 0
    t0, t2 = jnp.where(upper, t2, t0), jnp.where(upper, t0, t2)
    t1, t3 = jnp.where(upper, t3, t1), jnp.where(upper, t1, t3)
    return block_transpose((t0, t1, t2, t3), lane)


def chem_kernel(
    levels,
    width,
    quarter,
    entries,
    substeps,
    rank_ref,
    block0_ref,
    block1_ref,
    block2_ref,
    block3_ref,
    tail0_ref,
    tail1_ref,
    tail2_ref,
    tail3_ref,
    map_ref,
    last_ref,
    off_ref,
    keep_ref,
    give_ref,
    chem_ref,
):
    block_refs = (block0_ref, block1_ref, block2_ref, block3_ref)
    tail_refs = (tail0_ref, tail1_ref, tail2_ref, tail3_ref)
    parts = len(block_refs)
    species = parts * quarter
    half = width // 2
    even = (rank_ref[0, 0] & 1) == 0
    tables = tables_of(rank_ref[0, 0], [r[...] for r in tail_refs])
    columns = [jnp.where(even, tables[k], tables[half + k]) for k in range(half)]

    def row_of(index):
        return jnp.concatenate([columns[k][index : index + 1, :] for k in range(half)], axis=1)

    def block(part, group):
        return block_refs[part][group * quarter : (group + 1) * quarter, :]

    sun = substeps * levels
    lit = row_of(sun) > 0.0
    any_lit = jnp.max(row_of(sun)) > 0.0

    @pl.when(any_lit)
    def lit_tile():
        start = []
        for level in range(levels):
            cells = [
                jnp.concatenate([block(p, level * half + k) for p in range(parts)], axis=0)
                for k in range(half)
            ]
            start.append(jnp.concatenate(cells, axis=1))
        state = list(start)
        for step in range(substeps):
            final = step == substeps - 1
            rows = 2 * quarter if final else species
            matrix = last_ref[...] if final else map_ref[...]
            for level in range(levels):
                product = jnp.dot(matrix, state[level], preferred_element_type=F32)
                entry = row_of(step * levels + level)
                chosen = product[0:rows] + off_ref[0:rows, 0:1]
                for e in range(1, entries):
                    chosen = jnp.where(
                        entry == float(e),
                        product[e * rows : (e + 1) * rows] + off_ref[0:rows, e : e + 1],
                        chosen,
                    )
                chosen = jnp.maximum(chosen, 0.0)
                if not final:
                    state[level] = chosen.astype(BF16)
                    continue
                chem = jnp.where(lit, chosen, start[level][0:rows].astype(F32))
                for k in range(half):
                    chem_ref[level * half + k] = chem[:, k * LANES : (k + 1) * LANES]

    def solve(columns, source_of, out_ref):
        chunk = 32
        for k in range(half):
            pieces = [
                columns[k][sun + 1 + i * (levels - 1) : sun + 1 + (i + 1) * (levels - 1), :]
                for i in range(3)
            ]
            mixed = pieces[0] + pieces[1] + pieces[2]
            mixing = [mixed[i : i + 1, :] for i in range(levels - 1)]
            inverse, ratio = [], []
            for level in range(levels):
                diagonal = 1.0
                if level > 0:
                    diagonal = diagonal + mixing[level - 1]
                if level < levels - 1:
                    diagonal = diagonal + mixing[level]
                if level > 0:
                    diagonal = diagonal - mixing[level - 1] * ratio[level - 1]
                inverse.append(1.0 / diagonal)
                if level < levels - 1:
                    ratio.append(mixing[level] * inverse[level])
            for begin in range(0, quarter, chunk):
                solved = []
                for level in range(levels):
                    value = source_of(level * half + k, begin, chunk)
                    if level > 0:
                        value = value + mixing[level - 1] * solved[-1]
                    solved.append(value * inverse[level])
                for level in range(levels - 2, -1, -1):
                    solved[level] = solved[level] + ratio[level] * solved[level + 1]
                for level in range(levels):
                    place = begin * levels * half + level * half + k
                    out_ref[pl.ds(place, chunk, stride=levels * half), :] = solved[level]

    @pl.when(any_lit)
    def lit_mixing():
        for p, out_ref in enumerate((keep_ref, give_ref)):
            solve(
                columns,
                lambda g, begin, chunk: chem_ref[
                    g, p * quarter + begin : p * quarter + begin + chunk, :
                ],
                out_ref,
            )

    @pl.when(jnp.logical_not(any_lit))
    def dark_mixing():
        for ref, out_ref in ((block0_ref, keep_ref), (block1_ref, give_ref)):
            solve(
                columns,
                lambda g, begin, chunk: ref[
                    g * quarter + begin : g * quarter + begin + chunk, :
                ].astype(F32),
                out_ref,
            )


def keep_kernel(rank_ref, keep_ref, out_hbm, sem):
    copy = pltpu.make_async_copy(keep_ref, out_hbm.at[:, rank_ref[0, 0] & 1], sem)
    copy.start()
    copy.wait()


def fill_kernel(rank_ref, got_ref, part_hbm, out_hbm, sem):
    del part_hbm
    copy = pltpu.make_async_copy(got_ref, out_hbm.at[:, 1 - (rank_ref[0, 0] & 1)], sem)
    copy.start()
    copy.wait()


def shards(
    tracers,
    courant_cycle,
    courant_edge,
    seam_flags,
    sunlit,
    table_entry,
    linear_maps,
    offsets,
    mixing,
):
    quarter, levels, width, length = tracers.shape
    grid = levels * width
    substeps = table_entry.shape[0]
    entries, species, _ = linear_maps.shape
    count = lax.axis_size("tile")
    parts = lax.axis_size("trc")
    pairs = [(i, i ^ 1) for i in range(count)]
    seams = [(i, (i + (1 if i % 2 else -1)) % count) for i in range(count)]
    tile = lax.axis_index("tile").astype(jnp.int32).reshape(1, 1)
    halo = levels * 3 * quarter
    pieces = 4
    shape = jax.ShapeDtypeStruct
    brought = [
        tracers.reshape(quarter * grid, length),
        courant_cycle.reshape(grid, length),
        courant_edge.reshape(grid, length),
        table_entry,
        sunlit,
        mixing,
        seam_flags,
    ]
    to_a, to_b, x, cycle, edge, entry, sun, mix, flags = pl.pallas_call(
        functools.partial(pack_kernel, levels, width, quarter, pieces),
        out_shape=(
            shape((halo + 4 * levels, length), BF16),
            shape((halo + 4 * levels, length), BF16),
            *[shape(array.shape, array.dtype) for array in brought],
        ),
        in_specs=[smem()] + [hbm()] * len(brought),
        out_specs=(vmem(),) * (2 + len(brought)),
        scratch_shapes=[pltpu.SemaphoreType.DMA((pieces + len(brought) - 1,))],
        compiler_params=params(8),
        name="pack",
    )(tile, *[in_hbm(array) for array in brought])
    from_a0 = lax.ppermute(to_a, "tile", pairs[:2])
    from_b = lax.ppermute(to_b, "tile", seams)
    from_a1 = lax.ppermute(to_a, "tile", pairs[2:])
    rank = lax.axis_index("trc").astype(jnp.int32).reshape(1, 1)
    base, weights, table, turns = pl.pallas_call(
        functools.partial(local_kernel, levels, width, quarter),
        out_shape=(
            shape((grid, quarter, length), F32),
            shape((7, grid, length), F32),
            shape((TABLE_ROWS, length), BF16),
            shape((2, length, length), BF16),
        ),
        in_specs=[vmem()] * 7,
        out_specs=(vmem(),) * 4,
        scratch_shapes=[
            pltpu.VMEM((7, grid, length), F32),
            pltpu.VMEM((TABLE_ROWS, length), F32),
        ],
        compiler_params=params(8),
        cost_estimate=pl.CostEstimate(flops=4000000, bytes_accessed=1 << 20, transcendentals=0),
        name="local",
    )(
        flags,
        x,
        cycle,
        edge,
        entry.reshape(substeps * levels, length),
        sun.reshape(1, length),
        mix.reshape(levels - 1, length),
    )
    rows = grid // 2 * quarter
    near = pl.pallas_call(
        functools.partial(near_kernel, levels, width, quarter),
        out_shape=shape((grid, quarter, length), F32),
        in_specs=[smem()] + [vmem()] * 6,
        out_specs=vmem(),
        compiler_params=params(8),
        name="near",
    )(tile, x, base, weights, turns, from_a0, from_a1)
    mine, other = pl.pallas_call(
        functools.partial(flow_kernel, levels, width, quarter),
        out_shape=(shape((rows + TABLE_ROWS, length), BF16),) * 2,
        in_specs=[smem()] * 2 + [vmem()] * 6,
        out_specs=(vmem(),) * 2,
        compiler_params=params(8),
        name="flow",
    )(rank, tile, x, near, weights, table, turns, from_b)
    swap = {k: [(i, i ^ k) for i in range(parts)] for k in (1, 2, 3)}
    second = lax.ppermute(mine, "trc", swap[2])
    third = lax.ppermute(other, "trc", swap[3])
    first = lax.ppermute(other, "trc", swap[1])
    full, last, shift = pl.pallas_call(
        maps_kernel,
        out_shape=(
            shape((entries * parts, quarter, species), BF16),
            shape((2 * entries, quarter, species), BF16),
            shape((parts, quarter, entries), F32),
        ),
        in_specs=[smem()] + [vmem()] * 2,
        out_specs=(vmem(),) * 3,
        scratch_shapes=[pltpu.VMEM((entries * parts, quarter, species), BF16)],
        compiler_params=params(8),
        cost_estimate=pl.CostEstimate(flops=4000000, bytes_accessed=1 << 20, transcendentals=0),
        name="maps",
    )(rank, linear_maps, offsets.T.reshape(parts, quarter, entries))
    blocks = [mine, first, second, third]
    keep, give = pl.pallas_call(
        functools.partial(chem_kernel, levels, width, quarter, entries, substeps),
        out_shape=(shape((rows, length), F32),) * 2,
        in_specs=[smem()] + [vmem()] * 11,
        out_specs=(vmem(),) * 2,
        scratch_shapes=[pltpu.VMEM((grid // 2, 2 * quarter, length), F32)],
        compiler_params=params(24),
        name="chem",
    )(
        rank,
        *blocks,
        *[b[rows:] for b in blocks],
        full.reshape(entries * species, species),
        last.reshape(2 * entries * quarter, species),
        shift.reshape(species, entries),
    )
    got = lax.ppermute(give, "trc", swap[1])
    pair = (quarter * levels, width // 2, length)
    whole = shape((quarter * levels, 2, width // 2, length), F32)
    part = pl.pallas_call(
        keep_kernel,
        out_shape=whole,
        in_specs=[smem(), vmem()],
        out_specs=hbm(),
        scratch_shapes=[pltpu.SemaphoreType.DMA],
        compiler_params=params(4),
        cost_estimate=pl.CostEstimate(flops=1000000, bytes_accessed=1 << 19, transcendentals=0),
        name="keep",
    )(rank, keep.reshape(pair))
    out = pl.pallas_call(
        fill_kernel,
        out_shape=whole,
        in_specs=[smem(), vmem(), hbm()],
        out_specs=hbm(),
        scratch_shapes=[pltpu.SemaphoreType.DMA],
        input_output_aliases={2: 0},
        compiler_params=params(4),
        name="fill",
    )(rank, got.reshape(pair), part)
    return out.reshape(quarter, levels, width, length)


def solution(mesh):
    placed = (
        P("trc", None, "tile", None),
        P(None, "tile", None),
        P(None, "tile", None),
        P("tile", None),
        P("tile", "trc"),
        P(None, None, "tile", "trc"),
        P(),
        P(),
        P(None, "tile", "trc"),
    )
    return jax.shard_map(
        shards, mesh=mesh, in_specs=placed, out_specs=P("trc", None, "tile", None), check_vma=False
    )
```
